32 devices in a mesh: dp: 8 (over y, x, core), mp: 4 (over z).
Axes of the slice: x: 2, y: 2, z: 4, core: 2. Of those that a mesh axis runs over, the one named last changes fastest.
Arguments:
- tokens_in: bfloat16 [1024, 5120], P('dp'), may hold values from -6 to 6
- cotangent: bfloat16 [1024, 10240], P('dp', 'mp'), may hold values from -6 to 6
- old_weights: bfloat16 [112, 128, 128], P('mp'), may hold values from -0.25 to 0.25
- old_first: float32 [112, 16384], P('mp', 'dp'), may hold values from -6 to 6
- old_second: float32 [112, 16384], P('mp', 'dp'), may hold values from 0.25 to 4
- new_coords: int32 [80, 2], replicated, may hold values from 0 to 79, as said below
- moved_to: int32 [112], replicated, may hold values from -1 to 79, as said below
Outputs:
- activated: bfloat16 [1024, 10240], P('dp', 'mp')
- input_grads: bfloat16 [1024, 5120], P('dp', 'mp')
- new_weights: bfloat16 [80, 128, 128], P('mp')
- new_first: float32 [80, 16384], P('mp', 'dp')
- new_second: float32 [80, 16384], P('mp', 'dp')
The draws below stay inside these ranges and needn't reach their ends.
Inputs may be any that keep to these rules, and one draw needn't show every extreme that they name: new_coords[b] is (row block, column block) of new slot b, owned by mp index b // 20; no two slots share a cell. Call the column blocks of one index of mp a band; no owner has more than 11 blocks in one band, and in every draw some band holds exactly 11 blocks of every owner. moved_to[o] is the new slot that old slot o (held by mp index o // 28) moves to, or -1 where the old block is pruned or the slot is empty. Each new slot is named at most once; new slots that no old slot names are regrown. At most 7 blocks move from one old owner to one new owner; in every draw every new owner receives exactly 7 from some old owner, and some new owner receives 20 blocks in all.
All inputs are finite; a program needn't handle non-finite values.
Results may differ from the reference program's by a relative error of at most 0.0055.
Values may be sent and summed in bfloat16 or wider, within the bound.
No kernel may reach another device: no remote copies, remote signals or barrier semaphores. Data moves between devices by JAX's collectives and lax.ppermute only.
A program may use at most 64 MiB of HBM per device.

```python
import math
import jax
import jax.numpy as jnp
from jax import lax

D = 5120
FFW = 10240
BLK = 128
BLOCKS_PER_OWNER = 20
TOKENS = 1024
FSLOT = 11
MSLOT = 7
CAP = 28
OLD_SLOTS = 112
N_MP = 4


def block_layout(key):
    base_key = jax.random.fold_in(key, 4242)
    random_subkeys = jax.random.split(base_key, 9)
    row_blocks = D // BLK
    col_blocks = FFW // BLK
    band_width = col_blocks // N_MP
    total_blocks = N_MP * BLOCKS_PER_OWNER
    band_ids = jnp.arange(N_MP, dtype=jnp.int32)
    full_band = jax.random.randint(random_subkeys[0], (), 0, N_MP, dtype=jnp.int32)
    others = band_ids != full_band
    weights = jnp.where(others, jax.random.randint(random_subkeys[1], (N_MP,), 2, 4, dtype=jnp.int32), 0)
    remaining = N_MP * (BLOCKS_PER_OWNER - FSLOT)
    counts = remaining * weights // jnp.sum(weights)
    leftover = remaining - jnp.sum(counts)
    other_index = jnp.cumsum(others.astype(jnp.int32)) - 1
    counts = counts + jnp.where(others & (other_index < leftover), 1, 0)
    counts = jnp.where(others, counts, FSLOT * N_MP).astype(jnp.int32)
    band_ends = jnp.cumsum(counts).astype(jnp.int32)
    starts = band_ends - counts
    position = jnp.arange(total_blocks, dtype=jnp.int32)
    band_of = jnp.sum((position[:, None] >= band_ends[None, :]).astype(jnp.int32), axis=1)
    within = position - jnp.take(starts, band_of)
    cell_orders = jax.vmap(lambda subkey: jax.random.permutation(subkey, row_blocks * band_width))(jax.random.split(random_subkeys[2], N_MP)).astype(jnp.int32)
    cell_id = cell_orders[band_of, within]
    row_id = cell_id // band_width
    col_id = band_of * band_width + cell_id % band_width
    owner_of = position % N_MP
    slot_orders = jax.vmap(lambda subkey: jax.random.permutation(subkey, BLOCKS_PER_OWNER))(jax.random.split(random_subkeys[3], N_MP)).astype(jnp.int32)
    slot_id = slot_orders[owner_of, position // N_MP]
    global_slot = owner_of * BLOCKS_PER_OWNER + slot_id
    coords = jnp.zeros((total_blocks, 2), jnp.int32).at[global_slot].set(jnp.stack([row_id, col_id], axis=1).astype(jnp.int32))
    owner_indices = jnp.arange(N_MP, dtype=jnp.int32)
    persisting_blocks = jax.random.randint(random_subkeys[4], (N_MP,), BLOCKS_PER_OWNER - BLOCKS_PER_OWNER // 4, BLOCKS_PER_OWNER + 1, dtype=jnp.int32)
    complete_owner_list = jax.random.randint(random_subkeys[5], (), 0, N_MP, dtype=jnp.int32)
    persisting_blocks = jnp.where(owner_indices == complete_owner_list, BLOCKS_PER_OWNER, persisting_blocks)
    keep_orders = jax.vmap(lambda subkey: jax.random.permutation(subkey, BLOCKS_PER_OWNER))(jax.random.split(random_subkeys[6], N_MP)).astype(jnp.int32)
    shifts = jax.random.randint(random_subkeys[7], (N_MP,), 0, N_MP, dtype=jnp.int32)
    fresh_owner = position // BLOCKS_PER_OWNER
    retained_rank = keep_orders[fresh_owner, position % BLOCKS_PER_OWNER]
    block_persists = retained_rank < jnp.take(persisting_blocks, fresh_owner)
    old_owner = (fresh_owner + jnp.take(shifts, fresh_owner) + retained_rank // MSLOT) % N_MP
    order_key = fresh_owner * BLOCKS_PER_OWNER + retained_rank
    same_owner = (old_owner[None, :] == old_owner[:, None]) & block_persists[None, :] & (order_key[None, :] < order_key[:, None])
    old_rank = jnp.sum(same_owner.astype(jnp.int32), axis=1)
    old_orders = jax.vmap(lambda subkey: jax.random.permutation(subkey, CAP))(jax.random.split(random_subkeys[8], N_MP)).astype(jnp.int32)
    old_slot = old_orders[old_owner, jnp.minimum(old_rank, CAP - 1)]
    target = jnp.where(block_persists, old_owner * CAP + old_slot, N_MP * CAP)
    moved_list = jnp.full((N_MP * CAP,), -1, jnp.int32).at[target].set(position, mode='drop')
    return (coords, moved_list)


def draw_new_coords(key, part):
    return block_layout(key)[0]


def draw_moved_to(key, part):
    return block_layout(key)[1]


def levels(stream_key, dims, pieces, least, largest):
    factor_of, own = 1.0, jax.random.fold_in(stream_key, 6)
    for axis_at, parts in pieces:
        steps = jnp.exp(jax.random.uniform(jax.random.fold_in(own, axis_at), (parts,), jnp.float32, least / len(pieces), largest / len(pieces)))
        factor_of = factor_of * jnp.repeat(steps, dims[axis_at] // parts).reshape([-1 if axis == axis_at else 1 for axis in range(len(dims))])
    return factor_of


def normal_values(key, extent, deviation, bound, cuts=(), kind=jnp.bfloat16):
    drawn = deviation * jax.random.normal(key, extent, jnp.float32)
    if cuts:
        drawn = drawn * levels(key, extent, cuts, -0.22, 0.18)
    return jnp.clip(drawn, -bound, bound).astype(kind)


def setup_inputs(seed: int = 0) -> dict:
    streams_of = jax.random.split(jax.random.key(seed), 8)
    return {
        "tokens_in": normal_values(streams_of[0], (TOKENS, D), 1.0, 6.0, ((0, 8),)),
        "cotangent": normal_values(streams_of[1], (TOKENS, FFW), 1.0, 6.0, ((0, 8), (1, 4))),
        "old_weights": normal_values(streams_of[2], (OLD_SLOTS, BLK, BLK), (4 * BLK) ** -0.5, 0.25, ((0, 4),)),
        "old_first": normal_values(streams_of[3], (OLD_SLOTS, BLK * BLK), 1.0, 6.0, ((0, 4), (1, 8)), jnp.float32),
        "old_second": jnp.clip(jnp.exp(math.log(4.0) - 2.7725887 * jax.random.uniform(streams_of[4], (OLD_SLOTS, BLK * BLK), jnp.float32) ** levels(streams_of[4], (OLD_SLOTS, BLK * BLK), ((0, 4), (1, 8)), -0.2, 0.2)), 0.25, 4.0),
        "new_coords": draw_new_coords(jax.random.fold_in(streams_of[7], 71), 0),
        "moved_to": draw_moved_to(jax.random.fold_in(streams_of[7], 71), 0),
    }


BETA_ONE = 0.9
BETA_TWO = 0.95
LEARN_RATE = 0.01
ADAM_EPSILON = 0.05

def gelu_tanh(values):
    return jax.nn.gelu(values, approximate=True)

def reference(tokens_in, cotangent, old_weights, old_first, old_second, new_coords, moved_to):
    total_blocks = N_MP * BLOCKS_PER_OWNER
    old_total = N_MP * CAP
    targets = jnp.arange(total_blocks, dtype=jnp.int32)
    matches = moved_to[None, :] == targets[:, None]
    source = lax.optimization_barrier(jnp.sum(jnp.where(matches, jnp.arange(old_total, dtype=jnp.int32)[None, :], 0), axis=1)).astype(jnp.int32)
    arrived = jnp.any(matches, axis=1)
    weights_now = jnp.where(arrived[:, None, None], jnp.take(old_weights, source, axis=0), jnp.zeros((), jnp.bfloat16))
    first_now = jnp.where(arrived[:, None], jnp.take(old_first, source, axis=0), jnp.zeros((), jnp.float32))
    second_now = jnp.where(arrived[:, None], jnp.take(old_second, source, axis=0), jnp.zeros((), jnp.float32))
    row_ids = new_coords[:, 0].astype(jnp.int32)
    col_ids = new_coords[:, 1].astype(jnp.int32)
    token_blocks = tokens_in.reshape(TOKENS, D // BLK, BLK)
    zero_index = jnp.zeros((), jnp.int32)

    def forward_step(hidden, inputs):
        weight, row_id, col_id = inputs
        rows_in = lax.dynamic_index_in_dim(token_blocks, row_id, 1, keepdims=False)
        product = jnp.dot(rows_in, weight, preferred_element_type=jnp.float32).astype(jnp.bfloat16)
        product = lax.optimization_barrier(product).astype(jnp.float32)
        col_start = (col_id * BLK).astype(jnp.int32)
        current = lax.dynamic_slice(hidden, (zero_index, col_start), (TOKENS, BLK))
        return (lax.dynamic_update_slice(hidden, current + product, (zero_index, col_start)), None)
    hidden = lax.scan(forward_step, jnp.zeros((TOKENS, FFW), jnp.float32), (weights_now, row_ids, col_ids))[0]
    activated = gelu_tanh(hidden).astype(jnp.bfloat16)
    pullback = jax.vjp(gelu_tanh, hidden)[1]
    slopes = pullback(cotangent.astype(jnp.float32))[0].astype(jnp.bfloat16)

    def backward_step(grad_rows, inputs):
        weight, row_id, col_id = inputs
        rows_in = lax.dynamic_index_in_dim(token_blocks, row_id, 1, keepdims=False)
        col_start = (col_id * BLK).astype(jnp.int32)
        slope_cols = lax.dynamic_slice(slopes, (zero_index, col_start), (TOKENS, BLK))
        block_grad = jnp.dot(rows_in.T, slope_cols, preferred_element_type=jnp.float32)
        back_term = jnp.dot(slope_cols, weight.T, preferred_element_type=jnp.float32)
        row_start = (row_id * BLK).astype(jnp.int32)
        current = lax.dynamic_slice(grad_rows, (zero_index, row_start), (TOKENS, BLK))
        return (lax.dynamic_update_slice(grad_rows, current + back_term, (zero_index, row_start)), block_grad)
    grad_rows, block_grads = lax.scan(backward_step, jnp.zeros((TOKENS, D), jnp.float32), (weights_now, row_ids, col_ids))
    scaled_grads = block_grads.reshape(total_blocks, BLK * BLK) * (1.0 / math.sqrt(TOKENS))
    new_first = BETA_ONE * first_now + (1.0 - BETA_ONE) * scaled_grads
    new_second = BETA_TWO * second_now + (1.0 - BETA_TWO) * scaled_grads * scaled_grads
    flat_weights = weights_now.reshape(total_blocks, BLK * BLK).astype(jnp.float32)
    updated = flat_weights - LEARN_RATE * new_first / (jnp.sqrt(new_second) + ADAM_EPSILON)
    new_weights = updated.astype(jnp.bfloat16).reshape(total_blocks, BLK, BLK)
    return (activated, grad_rows.astype(jnp.bfloat16), new_weights, new_first, new_second)
```

```python
import functools
import math

import jax
import jax.numpy as jnp
from jax import lax
from jax.experimental import pallas as pl
from jax.experimental.pallas import tpu as pltpu
from jax.sharding import PartitionSpec as P

BETA_ONE = 0.9
BETA_TWO = 0.95
LEARN_RATE = 0.01
ADAM_EPSILON = 0.05
SQRT_2_OVER_PI = math.sqrt(2.0 / math.pi)


VMEM = pl.BlockSpec(memory_space=pltpu.VMEM)
SMEM = pl.BlockSpec(memory_space=pltpu.SMEM)


def call(kernel, out_shape, in_specs, out_specs, scratch, name):
    return pl.pallas_call(
        kernel,
        out_shape=out_shape,
        in_specs=in_specs,
        out_specs=out_specs,
        scratch_shapes=scratch,
        name=name,
    )


def shape(dims, dtype):
    return jax.ShapeDtypeStruct(dims, dtype)


def wrap(value, count):
    return jnp.where(value < 0, value + count, value)


def which_group(value, group, count):
    found = jnp.int32(0)
    for edge in range(1, count):
        found = found + (value >= edge * group).astype(jnp.int32)
    return found


def plan_kernel(cfg, here, coords, moved, first, second, *rest):
    n, per, cap, ms, bs, bw, pad = cfg
    table = rest[0]
    packs = rest[1 : 1 + n]
    src, out_slot, counts = rest[1 + n :]
    total = n * per
    slots = n * bs
    me = here[0]

    def fill(ref, base, size, value):
        def put(i, _):
            ref[base + i] = jnp.int32(value)
            return 0

        lax.fori_loop(0, size, put, 0)

    fill(src, 0, total, -1)
    fill(out_slot, 0, n * ms, 0)
    fill(table, 0, slots, -1)
    fill(table, slots, 2 * slots, 0)
    fill(table, 3 * slots, 3 * per, -1)

    for p in range(n):
        for i in range(n):
            counts[i] = jnp.int32(0)
        rel = wrap(me - p, n)

        def old_slot(j, _):
            o = p * cap + j
            t = moved[o]

            @pl.when(t >= 0)
            def _():
                dest = which_group(t, per, n)
                src[t] = rel * cap + j
                k = counts[dest]
                counts[dest] = k + 1

                @pl.when(me == p)
                def _():
                    out_slot[wrap(dest - me, n) * ms + k] = j

                @pl.when(dest == me)
                def _():
                    table[3 * slots + 2 * per + t - me * per] = rel * pad + k

            return 0

        lax.fori_loop(0, cap, old_slot, 0)

    for w in range(n):
        for i in range(n):
            counts[i] = jnp.int32(0)

        def new_slot(j, _):
            b = w * per + j
            col = coords[1, b]
            band = which_group(col, bw, n)
            k = counts[band]
            counts[band] = k + 1

            @pl.when(band == me)
            def _():
                q = w * bs + k
                table[q] = src[b]
                table[slots + q] = coords[0, b]
                table[2 * slots + q] = col - me * bw

            @pl.when(me == w)
            def _():
                table[3 * slots + j] = src[b]
                table[3 * slots + per + j] = wrap(me - band, n) * bs + k

            return 0

        lax.fori_loop(0, per, new_slot, 0)

    for s in range(n):
        for k in range(ms):
            row = out_slot[s * ms + k]
            packs[s][0, k : k + 1, :] = first[pl.ds(row, 1), :]
            packs[s][1, k : k + 1, :] = second[pl.ds(row, 1), :]
        if pad > ms:
            packs[s][:, ms:pad, :] = jnp.zeros((2, pad - ms, first.shape[1]), jnp.float32)


def select_kernel(cfg, table, *rest):
    n, per, cap, bs = cfg
    shares = rest[:n]
    picked, mine, pool = rest[n:]
    slots = n * bs
    for s in range(n):
        pool[s * cap : (s + 1) * cap] = shares[s][...]

    def pick(out, base):
        def one(i, _):
            at = table[base + i]
            row = pool[jnp.maximum(at, 0)]
            out[i] = jnp.where(at >= 0, row, jnp.zeros_like(row))
            return 0

        return one

    lax.fori_loop(0, slots, pick(picked, 0), 0, unroll=4)
    lax.fori_loop(0, per, pick(mine, 3 * slots), 0, unroll=4)


def forward_kernel(cfg, here, table, tokens, cotangent, *rest):
    n, bs, bw, blk, parts = cfg
    weights_in = rest[:parts]
    rest = rest[parts:]
    activated, slopes = rest[:2]
    far = rest[2 : 1 + n]
    own = rest[1 + n]
    weights, products, hidden, backs, grads = rest[2 + n :]
    slots = n * bs
    me = here[0]
    if parts == 1:
        weights = weights_in[0]
    else:
        rows = blk // parts
        d = here[1]
        for s in range(parts):
            weights[:, pl.ds(pl.multiple_of((d ^ s) * rows, rows), rows), :] = weights_in[s][...]

    def col_at(index):
        return pl.ds(pl.multiple_of(index * blk, blk), blk)

    def product(w, _):
        for k in range(bs):
            q = w * bs + k
            products[q] = jnp.dot(
                tokens[:, col_at(table[slots + q])],
                weights[q],
                preferred_element_type=jnp.float32,
            ).astype(jnp.bfloat16)
        return 0

    lax.fori_loop(0, n, product, 0)
    hidden[...] = jnp.zeros_like(hidden)

    def gather_hidden(q, _):
        at = col_at(table[2 * slots + q])
        hidden[:, at] = hidden[:, at] + products[q].astype(jnp.float32)
        return 0

    lax.fori_loop(0, slots, gather_hidden, 0)

    def pointwise(c, _):
        at = col_at(c)
        v = hidden[:, at]
        square = v * v
        t = jnp.tanh(SQRT_2_OVER_PI * (v + 0.044715 * (square * v)))
        half = 0.5 * (1.0 + t)
        activated[:, at] = (v * half).astype(jnp.bfloat16)
        slope = half + 0.5 * v * ((1.0 - t) * (1.0 + t)) * (
            SQRT_2_OVER_PI * (1.0 + (3.0 * 0.044715) * square)
        )
        slopes[:, at] = (cotangent[:, at].astype(jnp.float32) * slope).astype(jnp.bfloat16)
        return 0

    lax.fori_loop(0, bw, pointwise, 0)

    def back(w, _):
        for k in range(bs):
            q = w * bs + k
            backs[q] = lax.dot_general(
                slopes[:, col_at(table[2 * slots + q])],
                weights[q],
                (((1,), (1,)), ((), ())),
                preferred_element_type=jnp.float32,
            )
        return 0

    lax.fori_loop(0, n, back, 0)
    grads[...] = jnp.zeros_like(grads)

    def gather_back(q, _):
        at = col_at(table[slots + q])
        grads[:, at] = grads[:, at] + backs[q]
        return 0

    lax.fori_loop(0, slots, gather_back, 0)
    width = own.shape[1]

    def band_of(s):
        band = me + s
        band = jnp.where(band >= n, band - n, band)
        return grads[:, pl.ds(pl.multiple_of(band * width, blk), width)]

    own[...] = band_of(0)
    for s in range(1, n):
        far[s - 1][...] = band_of(s).astype(jnp.bfloat16)


def grad_kernel(cfg, here, table, tokens, slopes, *rest):
    n, bs, blk, parts = cfg
    outs = rest[:parts]
    partial = rest[parts]
    slots = n * bs

    def col_at(index):
        return pl.ds(pl.multiple_of(index * blk, blk), blk)

    target = outs[0] if parts == 1 else partial

    def one(w, _):
        for k in range(bs):
            q = w * bs + k
            target[q] = lax.dot_general(
                tokens[:, col_at(table[slots + q])],
                slopes[:, col_at(table[2 * slots + q])],
                (((0,), (0,)), ((), ())),
                preferred_element_type=jnp.float32,
            ).astype(jnp.bfloat16)
        return 0

    lax.fori_loop(0, n, one, 0)
    if parts > 1:
        rows = blk // parts
        d = here[1]
        for s in range(parts):
            outs[s][...] = partial[:, pl.ds(pl.multiple_of((d ^ s) * rows, rows), rows), :]


def pair_kernel(half, *refs):
    for j in range(half):
        total = refs[j][...].astype(jnp.float32) + refs[half + j][...].astype(jnp.float32)
        refs[2 * half + j][...] = total.astype(jnp.bfloat16)


def total_kernel(cfg, here, *rest):
    n, bs, count = cfg
    terms = rest[:count]
    outs = rest[count : count + n]
    pool = rest[count + n]
    me = here[0]
    total = terms[0][...].astype(jnp.float32)
    for term in terms[1:]:
        total = total + term[...].astype(jnp.float32)
    pool[...] = total.astype(jnp.bfloat16)
    for s in range(n):
        band = me + s
        band = jnp.where(band >= n, band - n, band)
        outs[s][...] = pool[pl.ds(band * bs, bs)]


def adam_kernel(cfg, table, mine, *rest):
    n, per, bs, pad, rows, scale = cfg
    grads = rest[:n]
    moments = rest[n : 2 * n]
    first_out, second_out, weight_out = rest[2 * n : 2 * n + 3]
    pool, moved, grad, weight, first, second = rest[2 * n + 3 :]
    slots = n * bs
    lanes = mine.shape[2]
    for s in range(n):
        pool[s * bs : (s + 1) * bs] = grads[s][...]
        moved[:, s * pad : (s + 1) * pad, :] = moments[s][...]

    for i in range(per):
        grad[i * rows : (i + 1) * rows, :] = (
            pool[table[3 * slots + per + i]].astype(jnp.float32) * scale
        )
        weight[i * rows : (i + 1) * rows, :] = mine[i].astype(jnp.float32)
        at = table[3 * slots + 2 * per + i]
        row = jnp.maximum(at, 0)
        old_first = moved[0, pl.ds(row, 1), :]
        old_second = moved[1, pl.ds(row, 1), :]
        first[i : i + 1, :] = jnp.where(at >= 0, old_first, jnp.zeros_like(old_first))
        second[i : i + 1, :] = jnp.where(at >= 0, old_second, jnp.zeros_like(old_second))

    for r in range(rows):
        at = slice(r * lanes, (r + 1) * lanes)
        strided = pl.ds(r, per, stride=rows)
        g = grad[strided, :]
        first_new = BETA_ONE * first[:, at] + (1.0 - BETA_ONE) * g
        second_new = BETA_TWO * second[:, at] + (1.0 - BETA_TWO) * g * g
        first_out[:, at] = first_new
        second_out[:, at] = second_new
        weight[strided, :] = weight[strided, :] - LEARN_RATE * first_new / (
            jnp.sqrt(second_new) + ADAM_EPSILON
        )
    for i in range(per):
        weight_out[i] = weight[i * rows : (i + 1) * rows, :].astype(jnp.bfloat16)


def join_kernel(parts, here, *rest):
    out = rest[parts]
    rows = rest[0].shape[1]
    d = here[1]
    for s in range(parts):
        out[:, pl.ds(pl.multiple_of((d ^ s) * rows, rows), rows), :] = rest[s][...]


def sum_kernel(own, *rest):
    total = own[...]
    for term in rest[:-1]:
        total = total + term[...].astype(jnp.float32)
    rest[-1][...] = total.astype(jnp.bfloat16)


def swap(value, bits, parts):
    return lax.ppermute(value, "dp", [(i, i ^ bits) for i in range(parts)])


def shift(value, step, n):
    return lax.ppermute(value, "mp", [(i, (i + step) % n) for i in range(n)])


def plane_gather(value, parts):
    pieces = [value] + [None] * (parts - 1)
    for s in range(2, parts, 2):
        pieces[s] = swap(value, s, parts)
    for s in range(0, parts, 2):
        pieces[s + 1] = swap(pieces[s], 1, parts)
    return pieces


def body(tokens_in, cotangent, old_weights, old_first, old_second, new_coords, moved_to):
    n = lax.axis_size("mp")
    parts = lax.axis_size("dp")
    me = lax.axis_index("mp")
    d = lax.axis_index("dp")
    cap, blk = old_weights.shape[:2]
    total = new_coords.shape[0]
    per = total // n
    shard = old_first.shape[1]
    rows = blk // parts
    tok, width = tokens_in.shape
    bw = cotangent.shape[1] // blk
    ms = cap // n
    pad = -(-ms // 8) * 8
    bs = 2 * per // n + 1
    slots = n * bs
    direct = rows % 16 == 0 and parts & (parts - 1) == 0
    bf16, f32 = jnp.bfloat16, jnp.float32
    here = jnp.stack([me, d]).astype(jnp.int32)

    share = lax.dynamic_slice_in_dim(old_weights, d * rows, rows, 1)
    shares = [share] + [shift(share, s, n) for s in range(1, n)]

    plan = call(
        functools.partial(plan_kernel, (n, per, cap, ms, bs, bw, pad)),
        [shape((3 * slots + 3 * per,), jnp.int32)] + [shape((2, pad, shard), f32)] * n,
        [SMEM, SMEM, SMEM, VMEM, VMEM],
        [SMEM] + [VMEM] * n,
        [
            pltpu.SMEM((total,), jnp.int32),
            pltpu.SMEM((n * ms,), jnp.int32),
            pltpu.SMEM((n,), jnp.int32),
        ],
        "plan",
    )(here, new_coords.T, moved_to, old_first, old_second)
    table, packs = plan[0], plan[1:]

    picked, mine = call(
        functools.partial(select_kernel, (n, per, cap, bs)),
        [shape((slots, rows, blk), bf16), shape((per, rows, blk), bf16)],
        [SMEM] + [VMEM] * n,
        [VMEM, VMEM],
        [pltpu.VMEM((n * cap, rows, blk), bf16)],
        "select",
    )(table, *shares)

    if direct:
        pieces = plane_gather(picked, parts)
    else:
        gathered = lax.all_gather(picked, "dp", axis=0)
        pieces = [gathered.transpose(1, 0, 2, 3).reshape(slots, blk, blk)]

    packs = list(lax.optimization_barrier(tuple(packs) + (picked,)))[:n]
    moments = [packs[0]] + [shift(packs[s], s, n) for s in range(1, n)]

    results = call(
        functools.partial(forward_kernel, (n, bs, bw, blk, len(pieces))),
        [shape((tok, bw * blk), bf16)] * 2
        + [shape((tok, width // n), bf16)] * (n - 1)
        + [shape((tok, width // n), f32)],
        [SMEM, SMEM, VMEM, VMEM] + [VMEM] * len(pieces),
        [VMEM] * (n + 2),
        [
            pltpu.VMEM((slots, blk, blk), bf16),
            pltpu.VMEM((slots, tok, blk), bf16),
            pltpu.VMEM((tok, bw * blk), f32),
            pltpu.VMEM((slots, tok, blk), f32),
            pltpu.VMEM((tok, width), f32),
        ],
        "forward",
    )(here, table, tokens_in, cotangent, *pieces)
    activated, slopes = results[:2]
    far, own = results[2 : 1 + n], results[1 + n]
    back_terms = [shift(far[s - 1], s, n) for s in range(1, n)]

    count = parts if direct else 1
    partials = call(
        functools.partial(grad_kernel, (n, bs, blk, count)),
        [shape((slots, blk // count, blk), bf16)] * count,
        [SMEM, SMEM, VMEM, VMEM],
        [VMEM] * count,
        [pltpu.VMEM((slots, blk, blk), bf16)],
        "grad",
    )(here, table, tokens_in, slopes)

    if direct:
        half = parts // 2
        even = [partials[2 * j] for j in range(half)]
        crossed = [swap(partials[2 * j + 1], 1, parts) for j in range(half)]
        paired = call(
            functools.partial(pair_kernel, half),
            [shape((slots, rows, blk), bf16)] * half,
            [VMEM] * parts,
            [VMEM] * half,
            [],
            "pair",
        )(*even, *crossed)
        terms = [paired[0]] + [swap(paired[j], 2 * j, parts) for j in range(1, half)]
    else:
        spread = partials[0].reshape(slots, parts, rows, blk).transpose(1, 0, 2, 3)
        spread = lax.all_to_all(spread, "dp", split_axis=0, concat_axis=0, tiled=True)
        terms = [jnp.sum(spread.astype(f32), axis=0)]

    owner_grads = call(
        functools.partial(total_kernel, (n, bs, len(terms))),
        [shape((bs, rows, blk), bf16)] * n,
        [SMEM] + [VMEM] * len(terms),
        [VMEM] * n,
        [pltpu.VMEM((slots, rows, blk), bf16)],
        "total",
    )(here, *terms)
    arrived = [owner_grads[0]] + [shift(owner_grads[s], s, n) for s in range(1, n)]

    first_new, second_new, weight_share = call(
        functools.partial(
            adam_kernel, (n, per, bs, pad, rows, 1.0 / math.sqrt(tok * parts))
        ),
        [shape((per, shard), f32)] * 2 + [shape((per, rows, blk), bf16)],
        [SMEM, VMEM] + [VMEM] * (2 * n),
        [VMEM] * 3,
        [
            pltpu.VMEM((slots, rows, blk), bf16),
            pltpu.VMEM((2, n * pad, shard), f32),
            pltpu.VMEM((per * rows, blk), f32),
            pltpu.VMEM((per * rows, blk), f32),
            pltpu.VMEM((per, shard), f32),
            pltpu.VMEM((per, shard), f32),
        ],
        "adam",
    )(table, mine, *arrived, *moments)

    if direct:
        weights_out = call(
            functools.partial(join_kernel, parts),
            shape((per, blk, blk), bf16),
            [SMEM] + [VMEM] * parts,
            VMEM,
            [],
            "join",
        )(here, *plane_gather(weight_share, parts))
    else:
        weights_out = lax.all_gather(weight_share, "dp", axis=1, tiled=True)

    grad_inputs = call(
        sum_kernel,
        shape((tok, width // n), bf16),
        [VMEM] * n,
        VMEM,
        [],
        "sum",
    )(own, *back_terms)
    return (activated, grad_inputs, weights_out, first_new, second_new)


def solution(mesh):
    in_specs = (
        P("dp", None),
        P("dp", "mp"),
        P("mp", None, None),
        P("mp", "dp"),
        P("mp", "dp"),
        P(),
        P(),
    )
    out_specs = (P("dp", "mp"), P("dp", "mp"), P("mp", None, None), P("mp", "dp"), P("mp", "dp"))
    return jax.shard_map(body, mesh=mesh, in_specs=in_specs, out_specs=out_specs, check_vma=False)
```

```python
import functools
import math

import jax
import jax.numpy as jnp
from jax import lax
from jax.experimental import pallas as pl
from jax.experimental.pallas import tpu as pltpu
from jax.sharding import PartitionSpec as P


BETA_ONE = 0.9
BETA_TWO = 0.95
LEARN_RATE = 0.01
ADAM_EPSILON = 0.05
SQRT_2_OVER_PI = math.sqrt(2.0 / math.pi)


VMEM = pl.BlockSpec(memory_space=pltpu.VMEM)
SMEM = pl.BlockSpec(memory_space=pltpu.SMEM)


def call(kernel, out_shape, in_specs, out_specs, scratch):
    return pl.pallas_call(
        kernel, out_shape=out_shape, in_specs=in_specs, out_specs=out_specs, scratch_shapes=scratch
    )


def shape(dims, dtype):
    return jax.ShapeDtypeStruct(dims, dtype)


def wrap(value, count):
    return jnp.where(value < 0, value + count, value)


def which_group(value, group, count):
    found = jnp.int32(0)
    for edge in range(1, count):
        found = found + (value >= edge * group).astype(jnp.int32)
    return found


def plan_kernel(cfg, here, coords, moved, first, second, *rest):
    n, per, cap, ms, bs, bw, pad = cfg
    table = rest[0]
    packs = rest[1 : 1 + n]
    src, out_slot, counts = rest[1 + n :]
    total = n * per
    slots = n * bs
    me = here[0]

    def fill(ref, base, size, value):
        def put(i, _):
            ref[base + i] = jnp.int32(value)
            return 0

        lax.fori_loop(0, size, put, 0)

    fill(src, 0, total, -1)
    fill(out_slot, 0, n * ms, 0)
    fill(table, 0, slots, -1)
    fill(table, slots, 2 * slots, 0)
    fill(table, 3 * slots, 3 * per, -1)

    for p in range(n):
        for i in range(n):
            counts[i] = jnp.int32(0)
        rel = wrap(me - p, n)

        def old_slot(j, _):
            o = p * cap + j
            t = moved[o]

            @pl.when(t >= 0)
            def _():
                dest = which_group(t, per, n)
                src[t] = rel * cap + j
                k = counts[dest]
                counts[dest] = k + 1

                @pl.when(me == p)
                def _():
                    out_slot[wrap(dest - me, n) * ms + k] = j

                @pl.when(dest == me)
                def _():
                    table[3 * slots + 2 * per + t - me * per] = rel * pad + k

            return 0

        lax.fori_loop(0, cap, old_slot, 0)

    for w in range(n):
        for i in range(n):
            counts[i] = jnp.int32(0)

        def new_slot(j, _):
            b = w * per + j
            col = coords[1, b]
            band = which_group(col, bw, n)
            k = counts[band]
            counts[band] = k + 1

            @pl.when(band == me)
            def _():
                q = w * bs + k
                table[q] = src[b]
                table[slots + q] = coords[0, b]
                table[2 * slots + q] = col - me * bw

            @pl.when(me == w)
            def _():
                table[3 * slots + j] = src[b]
                table[3 * slots + per + j] = wrap(me - band, n) * bs + k

            return 0

        lax.fori_loop(0, per, new_slot, 0)

    for s in range(n):
        for k in range(ms):
            row = out_slot[s * ms + k]
            packs[s][0, k : k + 1, :] = first[pl.ds(row, 1), :]
            packs[s][1, k : k + 1, :] = second[pl.ds(row, 1), :]
        if pad > ms:
            packs[s][:, ms:pad, :] = jnp.zeros((2, pad - ms, first.shape[1]), jnp.float32)


def select_kernel(cfg, table, *rest):
    n, per, cap, bs = cfg
    shares = rest[:n]
    picked, mine, pool = rest[n:]
    slots = n * bs
    for s in range(n):
        pool[s * cap : (s + 1) * cap] = shares[s][...]

    def pick(out, base):
        def one(i, _):
            at = table[base + i]
            row = pool[jnp.maximum(at, 0)]
            out[i] = jnp.where(at >= 0, row, jnp.zeros_like(row))
            return 0

        return one

    lax.fori_loop(0, slots, pick(picked, 0), 0, unroll=4)
    lax.fori_loop(0, per, pick(mine, 3 * slots), 0, unroll=4)


def forward_kernel(cfg, here, table, tokens, cotangent, *rest):
    n, bs, bw, blk, parts = cfg
    weights_in = rest[:parts]
    rest = rest[parts:]
    activated, slopes = rest[:2]
    far = rest[2 : 1 + n]
    own = rest[1 + n]
    weights, products, hidden, backs, grads = rest[2 + n :]
    slots = n * bs
    me = here[0]
    if parts == 1:
        weights = weights_in[0]
    else:
        rows = blk // parts
        d = here[1]
        for s in range(parts):
            weights[:, pl.ds(pl.multiple_of((d ^ s) * rows, rows), rows), :] = weights_in[s][...]

    def col_at(index):
        return pl.ds(pl.multiple_of(index * blk, blk), blk)

    def product(w, _):
        for k in range(bs):
            q = w * bs + k
            products[q] = jnp.dot(
                tokens[:, col_at(table[slots + q])],
                weights[q],
                preferred_element_type=jnp.float32,
            ).astype(jnp.bfloat16)
        return 0

    lax.fori_loop(0, n, product, 0)
    hidden[...] = jnp.zeros_like(hidden)

    def gather_hidden(q, _):
        at = col_at(table[2 * slots + q])
        hidden[:, at] = hidden[:, at] + products[q].astype(jnp.float32)
        return 0

    lax.fori_loop(0, slots, gather_hidden, 0)

    def pointwise(c, _):
        at = col_at(c)
        v = hidden[:, at]
        square = v * v
        t = jnp.tanh(SQRT_2_OVER_PI * (v + 0.044715 * (square * v)))
        half = 0.5 * (1.0 + t)
        activated[:, at] = (v * half).astype(jnp.bfloat16)
        slope = half + 0.5 * v * ((1.0 - t) * (1.0 + t)) * (
            SQRT_2_OVER_PI * (1.0 + (3.0 * 0.044715) * square)
        )
        slopes[:, at] = (cotangent[:, at].astype(jnp.float32) * slope).astype(jnp.bfloat16)
        return 0

    lax.fori_loop(0, bw, pointwise, 0)

    def back(w, _):
        for k in range(bs):
            q = w * bs + k
            backs[q] = lax.dot_general(
                slopes[:, col_at(table[2 * slots + q])],
                weights[q],
                (((1,), (1,)), ((), ())),
                preferred_element_type=jnp.float32,
            )
        return 0

    lax.fori_loop(0, n, back, 0)
    grads[...] = jnp.zeros_like(grads)

    def gather_back(q, _):
        at = col_at(table[slots + q])
        grads[:, at] = grads[:, at] + backs[q]
        return 0

    lax.fori_loop(0, slots, gather_back, 0)
    width = own.shape[1]

    def band_of(s):
        band = me + s
        band = jnp.where(band >= n, band - n, band)
        return grads[:, pl.ds(pl.multiple_of(band * width, blk), width)]

    own[...] = band_of(0)
    for s in range(1, n):
        far[s - 1][...] = band_of(s).astype(jnp.bfloat16)


def grad_kernel(cfg, here, table, tokens, slopes, *rest):
    n, bs, blk, parts = cfg
    outs = rest[:parts]
    partial = rest[parts]
    slots = n * bs

    def col_at(index):
        return pl.ds(pl.multiple_of(index * blk, blk), blk)

    target = outs[0] if parts == 1 else partial

    def one(w, _):
        for k in range(bs):
            q = w * bs + k
            target[q] = lax.dot_general(
                tokens[:, col_at(table[slots + q])],
                slopes[:, col_at(table[2 * slots + q])],
                (((0,), (0,)), ((), ())),
                preferred_element_type=jnp.float32,
            ).astype(jnp.bfloat16)
        return 0

    lax.fori_loop(0, n, one, 0)
    if parts > 1:
        rows = blk // parts
        d = here[1]
        for s in range(parts):
            outs[s][...] = partial[:, pl.ds(pl.multiple_of((d ^ s) * rows, rows), rows), :]


def pair_kernel(half, *refs):
    for j in range(half):
        total = refs[j][...].astype(jnp.float32) + refs[half + j][...].astype(jnp.float32)
        refs[2 * half + j][...] = total.astype(jnp.bfloat16)


def total_kernel(cfg, here, *rest):
    n, bs, count = cfg
    terms = rest[:count]
    outs = rest[count : count + n]
    pool = rest[count + n]
    me = here[0]
    total = terms[0][...].astype(jnp.float32)
    for term in terms[1:]:
        total = total + term[...].astype(jnp.float32)
    pool[...] = total.astype(jnp.bfloat16)
    for s in range(n):
        band = me + s
        band = jnp.where(band >= n, band - n, band)
        outs[s][...] = pool[pl.ds(band * bs, bs)]


def adam_kernel(cfg, table, mine, *rest):
    n, per, bs, pad, rows, scale = cfg
    grads = rest[:n]
    moments = rest[n : 2 * n]
    first_out, second_out, weight_out = rest[2 * n : 2 * n + 3]
    pool, moved, grad, weight, first, second = rest[2 * n + 3 :]
    slots = n * bs
    lanes = mine.shape[2]
    for s in range(n):
        pool[s * bs : (s + 1) * bs] = grads[s][...]
        moved[:, s * pad : (s + 1) * pad, :] = moments[s][...]

    for i in range(per):
        grad[i * rows : (i + 1) * rows, :] = (
            pool[table[3 * slots + per + i]].astype(jnp.float32) * scale
        )
        weight[i * rows : (i + 1) * rows, :] = mine[i].astype(jnp.float32)
        at = table[3 * slots + 2 * per + i]
        row = jnp.maximum(at, 0)
        old_first = moved[0, pl.ds(row, 1), :]
        old_second = moved[1, pl.ds(row, 1), :]
        first[i : i + 1, :] = jnp.where(at >= 0, old_first, jnp.zeros_like(old_first))
        second[i : i + 1, :] = jnp.where(at >= 0, old_second, jnp.zeros_like(old_second))

    for r in range(rows):
        at = slice(r * lanes, (r + 1) * lanes)
        strided = pl.ds(r, per, stride=rows)
        g = grad[strided, :]
        first_new = BETA_ONE * first[:, at] + (1.0 - BETA_ONE) * g
        second_new = BETA_TWO * second[:, at] + (1.0 - BETA_TWO) * g * g
        first_out[:, at] = first_new
        second_out[:, at] = second_new
        weight[strided, :] = weight[strided, :] - LEARN_RATE * first_new / (
            jnp.sqrt(second_new) + ADAM_EPSILON
        )
    for i in range(per):
        weight_out[i] = weight[i * rows : (i + 1) * rows, :].astype(jnp.bfloat16)


def join_kernel(parts, here, *rest):
    out = rest[parts]
    rows = rest[0].shape[1]
    d = here[1]
    for s in range(parts):
        out[:, pl.ds(pl.multiple_of((d ^ s) * rows, rows), rows), :] = rest[s][...]


def sum_kernel(own, *rest):
    total = own[...]
    for term in rest[:-1]:
        total = total + term[...].astype(jnp.float32)
    rest[-1][...] = total.astype(jnp.bfloat16)


def swap(value, bits, parts):
    return lax.ppermute(value, "dp", [(i, i ^ bits) for i in range(parts)])


def shift(value, step, n):
    return lax.ppermute(value, "mp", [(i, (i + step) % n) for i in range(n)])


def plane_gather(value, parts):
    pieces = [value] + [None] * (parts - 1)
    for s in range(2, parts, 2):
        pieces[s] = swap(value, s, parts)
    for s in range(0, parts, 2):
        pieces[s + 1] = swap(pieces[s], 1, parts)
    return pieces


def step(tokens_in, cotangent, old_weights, old_first, old_second, new_coords, moved_to):
    n = lax.axis_size("mp")
    parts = lax.axis_size("dp")
    me = lax.axis_index("mp")
    d = lax.axis_index("dp")
    cap, blk = old_weights.shape[:2]
    total = new_coords.shape[0]
    per = total // n
    shard = old_first.shape[1]
    rows = blk // parts
    tok, width = tokens_in.shape
    bw = cotangent.shape[1] // blk
    ms = cap // n
    pad = -(-ms // 8) * 8
    bs = 2 * per // n + 1
    slots = n * bs
    direct = rows % 16 == 0 and parts & (parts - 1) == 0
    bf16, f32 = jnp.bfloat16, jnp.float32
    here = jnp.stack([me, d]).astype(jnp.int32)

    share = lax.dynamic_slice_in_dim(old_weights, d * rows, rows, 1)
    shares = [share] + [shift(share, s, n) for s in range(1, n)]

    plan = call(
        functools.partial(plan_kernel, (n, per, cap, ms, bs, bw, pad)),
        [shape((3 * slots + 3 * per,), jnp.int32)] + [shape((2, pad, shard), f32)] * n,
        [SMEM, SMEM, SMEM, VMEM, VMEM],
        [SMEM] + [VMEM] * n,
        [
            pltpu.SMEM((total,), jnp.int32),
            pltpu.SMEM((n * ms,), jnp.int32),
            pltpu.SMEM((n,), jnp.int32),
        ],
    )(here, new_coords.T, moved_to, old_first, old_second)
    table, packs = plan[0], plan[1:]

    picked, mine = call(
        functools.partial(select_kernel, (n, per, cap, bs)),
        [shape((slots, rows, blk), bf16), shape((per, rows, blk), bf16)],
        [SMEM] + [VMEM] * n,
        [VMEM, VMEM],
        [pltpu.VMEM((n * cap, rows, blk), bf16)],
    )(table, *shares)

    if direct:
        pieces = plane_gather(picked, parts)
    else:
        gathered = lax.all_gather(picked, "dp", axis=0)
        pieces = [gathered.transpose(1, 0, 2, 3).reshape(slots, blk, blk)]

    packs = list(lax.optimization_barrier(tuple(packs) + (picked,)))[:n]
    moments = [packs[0]] + [shift(packs[s], s, n) for s in range(1, n)]

    results = call(
        functools.partial(forward_kernel, (n, bs, bw, blk, len(pieces))),
        [shape((tok, bw * blk), bf16)] * 2
        + [shape((tok, width // n), bf16)] * (n - 1)
        + [shape((tok, width // n), f32)],
        [SMEM, SMEM, VMEM, VMEM] + [VMEM] * len(pieces),
        [VMEM] * (n + 2),
        [
            pltpu.VMEM((slots, blk, blk), bf16),
            pltpu.VMEM((slots, tok, blk), bf16),
            pltpu.VMEM((tok, bw * blk), f32),
            pltpu.VMEM((slots, tok, blk), f32),
            pltpu.VMEM((tok, width), f32),
        ],
    )(here, table, tokens_in, cotangent, *pieces)
    activated, slopes = results[:2]
    far, own = results[2 : 1 + n], results[1 + n]
    back_terms = [shift(far[s - 1], s, n) for s in range(1, n)]

    count = parts if direct else 1
    partials = call(
        functools.partial(grad_kernel, (n, bs, blk, count)),
        [shape((slots, blk // count, blk), bf16)] * count,
        [SMEM, SMEM, VMEM, VMEM],
        [VMEM] * count,
        [pltpu.VMEM((slots, blk, blk), bf16)],
    )(here, table, tokens_in, slopes)

    if direct:
        half = parts // 2
        even = [partials[2 * j] for j in range(half)]
        crossed = [swap(partials[2 * j + 1], 1, parts) for j in range(half)]
        paired = call(
            functools.partial(pair_kernel, half),
            [shape((slots, rows, blk), bf16)] * half,
            [VMEM] * parts,
            [VMEM] * half,
            [],
        )(*even, *crossed)
        terms = [paired[0]] + [swap(paired[j], 2 * j, parts) for j in range(1, half)]
    else:
        spread = partials[0].reshape(slots, parts, rows, blk).transpose(1, 0, 2, 3)
        spread = lax.all_to_all(spread, "dp", split_axis=0, concat_axis=0, tiled=True)
        terms = [jnp.sum(spread.astype(f32), axis=0)]

    owner_grads = call(
        functools.partial(total_kernel, (n, bs, len(terms))),
        [shape((bs, rows, blk), bf16)] * n,
        [SMEM] + [VMEM] * len(terms),
        [VMEM] * n,
        [pltpu.VMEM((slots, rows, blk), bf16)],
    )(here, *terms)
    arrived = [owner_grads[0]] + [shift(owner_grads[s], s, n) for s in range(1, n)]

    first_new, second_new, weight_share = call(
        functools.partial(
            adam_kernel, (n, per, bs, pad, rows, 1.0 / math.sqrt(tok * parts))
        ),
        [shape((per, shard), f32)] * 2 + [shape((per, rows, blk), bf16)],
        [SMEM, VMEM] + [VMEM] * (2 * n),
        [VMEM] * 3,
        [
            pltpu.VMEM((slots, rows, blk), bf16),
            pltpu.VMEM((2, n * pad, shard), f32),
            pltpu.VMEM((per * rows, blk), f32),
            pltpu.VMEM((per * rows, blk), f32),
            pltpu.VMEM((per, shard), f32),
            pltpu.VMEM((per, shard), f32),
        ],
    )(table, mine, *arrived, *moments)

    if direct:
        weights_out = call(
            functools.partial(join_kernel, parts),
            shape((per, blk, blk), bf16),
            [SMEM] + [VMEM] * parts,
            VMEM,
            [],
        )(here, *plane_gather(weight_share, parts))
    else:
        weights_out = lax.all_gather(weight_share, "dp", axis=1, tiled=True)

    grad_inputs = call(
        sum_kernel, shape((tok, width // n), bf16), [VMEM] * n, VMEM, []
    )(own, *back_terms)
    return (activated, grad_inputs, weights_out, first_new, second_new)


def solution(mesh):
    in_specs = (
        P("dp", None),
        P("dp", "mp"),
        P("mp", None, None),
        P("mp", "dp"),
        P("mp", "dp"),
        P(),
        P(),
    )
    out_specs = (P("dp", "mp"), P("dp", "mp"), P("mp", None, None), P("mp", "dp"), P("mp", "dp"))
    return jax.shard_map(step, mesh=mesh, in_specs=in_specs, out_specs=out_specs, check_vma=False)
```

```python
import functools
import math

import jax
import jax.numpy as jnp
from jax import lax
from jax.experimental import pallas as pl
from jax.experimental.pallas import tpu as pltpu
from jax.sharding import PartitionSpec as P


BETA_ONE = 0.9
BETA_TWO = 0.95
LEARN_RATE = 0.01
ADAM_EPSILON = 0.05
SQRT_2_OVER_PI = math.sqrt(2.0 / math.pi)


ROOM_BYTES = 4 << 20

VMEM = pl.BlockSpec(memory_space=pltpu.VMEM)
SMEM = pl.BlockSpec(memory_space=pltpu.SMEM)


def size_of(item):
    return math.prod(item.shape) * jnp.dtype(item.dtype).itemsize


def call(kernel, out_shape, in_specs, out_specs, scratch):
    def run(*args):
        outs = out_shape if isinstance(out_shape, list) else [out_shape]
        room = sum(size_of(x) for x in (*args, *outs)) + sum(size_of(x) for x in scratch)
        return pl.pallas_call(
            kernel,
            out_shape=out_shape,
            in_specs=in_specs,
            out_specs=out_specs,
            scratch_shapes=scratch,
            compiler_params=pltpu.CompilerParams(vmem_limit_bytes=room + ROOM_BYTES),
        )(*args)

    return run


def shape(dims, dtype):
    return jax.ShapeDtypeStruct(dims, dtype)


def wrap(value, count):
    return jnp.where(value < 0, value + count, value)


def which_group(value, group, count):
    found = jnp.int32(0)
    for edge in range(1, count):
        found = found + (value >= edge * group).astype(jnp.int32)
    return found


def plan_kernel(cfg, here, coords, moved, first, second, *rest):
    n, per, cap, ms, bs, bw, pad = cfg
    table = rest[0]
    packs = rest[1 : 1 + n]
    src, out_slot, counts = rest[1 + n :]
    total = n * per
    slots = n * bs
    me = here[0]

    def fill(ref, base, size, value):
        def put(i, _):
            ref[base + i] = jnp.int32(value)
            return 0

        lax.fori_loop(0, size, put, 0)

    fill(src, 0, total, -1)
    fill(out_slot, 0, n * ms, 0)
    fill(table, 0, slots, -1)
    fill(table, slots, 2 * slots, 0)
    fill(table, 3 * slots, 3 * per, -1)

    for p in range(n):
        for i in range(n):
            counts[i] = jnp.int32(0)
        rel = wrap(me - p, n)

        def old_slot(j, _):
            o = p * cap + j
            t = moved[o]

            @pl.when(t >= 0)
            def _():
                dest = which_group(t, per, n)
                src[t] = rel * cap + j
                k = counts[dest]
                counts[dest] = k + 1

                @pl.when(me == p)
                def _():
                    out_slot[wrap(dest - me, n) * ms + k] = j

                @pl.when(dest == me)
                def _():
                    table[3 * slots + 2 * per + t - me * per] = rel * pad + k

            return 0

        lax.fori_loop(0, cap, old_slot, 0)

    for w in range(n):
        for i in range(n):
            counts[i] = jnp.int32(0)

        def new_slot(j, _):
            b = w * per + j
            col = coords[1, b]
            band = which_group(col, bw, n)
            k = counts[band]
            counts[band] = k + 1

            @pl.when(band == me)
            def _():
                q = w * bs + k
                table[q] = src[b]
                table[slots + q] = coords[0, b]
                table[2 * slots + q] = col - me * bw

            @pl.when(me == w)
            def _():
                table[3 * slots + j] = src[b]
                table[3 * slots + per + j] = wrap(me - band, n) * bs + k

            return 0

        lax.fori_loop(0, per, new_slot, 0)

    for s in range(n):
        for k in range(ms):
            row = out_slot[s * ms + k]
            packs[s][0, k : k + 1, :] = first[pl.ds(row, 1), :]
            packs[s][1, k : k + 1, :] = second[pl.ds(row, 1), :]
        if pad > ms:
            packs[s][:, ms:pad, :] = jnp.zeros((2, pad - ms, first.shape[1]), jnp.float32)


def select_kernel(cfg, table, *rest):
    n, per, cap, bs = cfg
    shares = rest[:n]
    picked, mine, pool = rest[n:]
    slots = n * bs
    for s in range(n):
        pool[s * cap : (s + 1) * cap] = shares[s][...]

    def pick(out, base):
        def one(i, _):
            at = table[base + i]
            row = pool[jnp.maximum(at, 0)]
            out[i] = jnp.where(at >= 0, row, jnp.zeros_like(row))
            return 0

        return one

    lax.fori_loop(0, slots, pick(picked, 0), 0, unroll=4)
    lax.fori_loop(0, per, pick(mine, 3 * slots), 0, unroll=4)


def forward_kernel(cfg, here, table, tokens, cotangent, *rest):
    n, bs, bw, blk, parts = cfg
    weights_in = rest[:parts]
    rest = rest[parts:]
    activated, slopes = rest[:2]
    far = rest[2 : 1 + n]
    own = rest[1 + n]
    weights, products, hidden, backs, grads = rest[2 + n :]
    slots = n * bs
    me = here[0]
    if parts == 1:
        weights = weights_in[0]
    else:
        rows = blk // parts
        d = here[1]
        for s in range(parts):
            weights[:, pl.ds(pl.multiple_of((d ^ s) * rows, rows), rows), :] = weights_in[s][...]

    def col_at(index):
        return pl.ds(pl.multiple_of(index * blk, blk), blk)

    def product(w, _):
        for k in range(bs):
            q = w * bs + k
            products[q] = jnp.dot(
                tokens[:, col_at(table[slots + q])],
                weights[q],
                preferred_element_type=jnp.float32,
            ).astype(jnp.bfloat16)
        return 0

    lax.fori_loop(0, n, product, 0)
    hidden[...] = jnp.zeros_like(hidden)

    def gather_hidden(q, _):
        at = col_at(table[2 * slots + q])
        hidden[:, at] = hidden[:, at] + products[q].astype(jnp.float32)
        return 0

    lax.fori_loop(0, slots, gather_hidden, 0)

    def pointwise(c, _):
        at = col_at(c)
        v = hidden[:, at]
        square = v * v
        t = jnp.tanh(SQRT_2_OVER_PI * (v + 0.044715 * (square * v)))
        half = 0.5 * (1.0 + t)
        activated[:, at] = (v * half).astype(jnp.bfloat16)
        slope = half + 0.5 * v * ((1.0 - t) * (1.0 + t)) * (
            SQRT_2_OVER_PI * (1.0 + (3.0 * 0.044715) * square)
        )
        slopes[:, at] = (cotangent[:, at].astype(jnp.float32) * slope).astype(jnp.bfloat16)
        return 0

    lax.fori_loop(0, bw, pointwise, 0)

    def back(w, _):
        for k in range(bs):
            q = w * bs + k
            backs[q] = lax.dot_general(
                slopes[:, col_at(table[2 * slots + q])],
                weights[q],
                (((1,), (1,)), ((), ())),
                preferred_element_type=jnp.float32,
            )
        return 0

    lax.fori_loop(0, n, back, 0)
    grads[...] = jnp.zeros_like(grads)

    def gather_back(q, _):
        at = col_at(table[slots + q])
        grads[:, at] = grads[:, at] + backs[q]
        return 0

    lax.fori_loop(0, slots, gather_back, 0)
    width = own.shape[1]

    def band_of(s):
        band = me + s
        band = jnp.where(band >= n, band - n, band)
        return grads[:, pl.ds(pl.multiple_of(band * width, blk), width)]

    own[...] = band_of(0)
    for s in range(1, n):
        far[s - 1][...] = band_of(s).astype(jnp.bfloat16)


def grad_kernel(cfg, here, table, tokens, slopes, *rest):
    n, bs, blk, parts = cfg
    outs = rest[:parts]
    partial = rest[parts]
    slots = n * bs

    def col_at(index):
        return pl.ds(pl.multiple_of(index * blk, blk), blk)

    target = outs[0] if parts == 1 else partial

    def one(w, _):
        for k in range(bs):
            q = w * bs + k
            target[q] = lax.dot_general(
                tokens[:, col_at(table[slots + q])],
                slopes[:, col_at(table[2 * slots + q])],
                (((0,), (0,)), ((), ())),
                preferred_element_type=jnp.float32,
            ).astype(jnp.bfloat16)
        return 0

    lax.fori_loop(0, n, one, 0)
    if parts > 1:
        rows = blk // parts
        d = here[1]
        for s in range(parts):
            outs[s][...] = partial[:, pl.ds(pl.multiple_of((d ^ s) * rows, rows), rows), :]


def pair_kernel(half, *refs):
    for j in range(half):
        total = refs[j][...].astype(jnp.float32) + refs[half + j][...].astype(jnp.float32)
        refs[2 * half + j][...] = total.astype(jnp.bfloat16)


def total_kernel(cfg, here, *rest):
    n, bs, count = cfg
    terms = rest[:count]
    outs = rest[count : count + n]
    pool = rest[count + n]
    me = here[0]
    total = terms[0][...].astype(jnp.float32)
    for term in terms[1:]:
        total = total + term[...].astype(jnp.float32)
    pool[...] = total.astype(jnp.bfloat16)
    for s in range(n):
        band = me + s
        band = jnp.where(band >= n, band - n, band)
        outs[s][...] = pool[pl.ds(band * bs, bs)]


def adam_kernel(cfg, table, mine, *rest):
    n, per, bs, pad, rows, scale = cfg
    grads = rest[:n]
    moments = rest[n : 2 * n]
    first_out, second_out, weight_out = rest[2 * n : 2 * n + 3]
    pool, moved, grad, weight, first, second = rest[2 * n + 3 :]
    slots = n * bs
    lanes = mine.shape[2]
    for s in range(n):
        pool[s * bs : (s + 1) * bs] = grads[s][...]
        moved[:, s * pad : (s + 1) * pad, :] = moments[s][...]

    for i in range(per):
        grad[i * rows : (i + 1) * rows, :] = (
            pool[table[3 * slots + per + i]].astype(jnp.float32) * scale
        )
        weight[i * rows : (i + 1) * rows, :] = mine[i].astype(jnp.float32)
        at = table[3 * slots + 2 * per + i]
        row = jnp.maximum(at, 0)
        old_first = moved[0, pl.ds(row, 1), :]
        old_second = moved[1, pl.ds(row, 1), :]
        first[i : i + 1, :] = jnp.where(at >= 0, old_first, jnp.zeros_like(old_first))
        second[i : i + 1, :] = jnp.where(at >= 0, old_second, jnp.zeros_like(old_second))

    for r in range(rows):
        at = slice(r * lanes, (r + 1) * lanes)
        strided = pl.ds(r, per, stride=rows)
        g = grad[strided, :]
        first_new = BETA_ONE * first[:, at] + (1.0 - BETA_ONE) * g
        second_new = BETA_TWO * second[:, at] + (1.0 - BETA_TWO) * g * g
        first_out[:, at] = first_new
        second_out[:, at] = second_new
        weight[strided, :] = weight[strided, :] - LEARN_RATE * first_new / (
            jnp.sqrt(second_new) + ADAM_EPSILON
        )
    for i in range(per):
        weight_out[i] = weight[i * rows : (i + 1) * rows, :].astype(jnp.bfloat16)


def join_kernel(parts, here, *rest):
    out = rest[parts]
    rows = rest[0].shape[1]
    d = here[1]
    for s in range(parts):
        out[:, pl.ds(pl.multiple_of((d ^ s) * rows, rows), rows), :] = rest[s][...]


def sum_kernel(own, *rest):
    total = own[...]
    for term in rest[:-1]:
        total = total + term[...].astype(jnp.float32)
    rest[-1][...] = total.astype(jnp.bfloat16)


def swap(value, bits, parts):
    return lax.ppermute(value, "dp", [(i, i ^ bits) for i in range(parts)])


def shift(value, step, n):
    return lax.ppermute(value, "mp", [(i, (i + step) % n) for i in range(n)])


def plane_gather(value, parts):
    pieces = [value] + [None] * (parts - 1)
    for s in range(2, parts, 2):
        pieces[s] = swap(value, s, parts)
    for s in range(0, parts, 2):
        pieces[s + 1] = swap(pieces[s], 1, parts)
    return pieces


def step(tokens_in, cotangent, old_weights, old_first, old_second, new_coords, moved_to):
    n = lax.axis_size("mp")
    parts = lax.axis_size("dp")
    me = lax.axis_index("mp")
    d = lax.axis_index("dp")
    cap, blk = old_weights.shape[:2]
    total = new_coords.shape[0]
    per = total // n
    shard = old_first.shape[1]
    rows = blk // parts
    tok, width = tokens_in.shape
    bw = cotangent.shape[1] // blk
    ms = cap // n
    pad = -(-ms // 8) * 8
    bs = 2 * per // n + 1
    slots = n * bs
    direct = rows % 16 == 0 and parts & (parts - 1) == 0
    bf16, f32 = jnp.bfloat16, jnp.float32
    here = jnp.stack([me, d]).astype(jnp.int32)

    share = lax.dynamic_slice_in_dim(old_weights, d * rows, rows, 1)
    shares = [share] + [shift(share, s, n) for s in range(1, n)]

    plan = call(
        functools.partial(plan_kernel, (n, per, cap, ms, bs, bw, pad)),
        [shape((3 * slots + 3 * per,), jnp.int32)] + [shape((2, pad, shard), f32)] * n,
        [SMEM, SMEM, SMEM, VMEM, VMEM],
        [SMEM] + [VMEM] * n,
        [
            pltpu.SMEM((total,), jnp.int32),
            pltpu.SMEM((n * ms,), jnp.int32),
            pltpu.SMEM((n,), jnp.int32),
        ],
    )(here, new_coords.T, moved_to, old_first, old_second)
    table, packs = plan[0], plan[1:]

    picked, mine = call(
        functools.partial(select_kernel, (n, per, cap, bs)),
        [shape((slots, rows, blk), bf16), shape((per, rows, blk), bf16)],
        [SMEM] + [VMEM] * n,
        [VMEM, VMEM],
        [pltpu.VMEM((n * cap, rows, blk), bf16)],
    )(table, *shares)

    if direct:
        pieces = plane_gather(picked, parts)
    else:
        gathered = lax.all_gather(picked, "dp", axis=0)
        pieces = [gathered.transpose(1, 0, 2, 3).reshape(slots, blk, blk)]

    packs = list(lax.optimization_barrier(tuple(packs) + (picked,)))[:n]
    moments = [packs[0]] + [shift(packs[s], s, n) for s in range(1, n)]

    results = call(
        functools.partial(forward_kernel, (n, bs, bw, blk, len(pieces))),
        [shape((tok, bw * blk), bf16)] * 2
        + [shape((tok, width // n), bf16)] * (n - 1)
        + [shape((tok, width // n), f32)],
        [SMEM, SMEM, VMEM, VMEM] + [VMEM] * len(pieces),
        [VMEM] * (n + 2),
        [
            pltpu.VMEM((slots, blk, blk), bf16),
            pltpu.VMEM((slots, tok, blk), bf16),
            pltpu.VMEM((tok, bw * blk), f32),
            pltpu.VMEM((slots, tok, blk), f32),
            pltpu.VMEM((tok, width), f32),
        ],
    )(here, table, tokens_in, cotangent, *pieces)
    activated, slopes = results[:2]
    far, own = results[2 : 1 + n], results[1 + n]
    back_terms = [shift(far[s - 1], s, n) for s in range(1, n)]

    count = parts if direct else 1
    partials = call(
        functools.partial(grad_kernel, (n, bs, blk, count)),
        [shape((slots, blk // count, blk), bf16)] * count,
        [SMEM, SMEM, VMEM, VMEM],
        [VMEM] * count,
        [pltpu.VMEM((slots, blk, blk), bf16)],
    )(here, table, tokens_in, slopes)

    if direct:
        half = parts // 2
        even = [partials[2 * j] for j in range(half)]
        crossed = [swap(partials[2 * j + 1], 1, parts) for j in range(half)]
        paired = call(
            functools.partial(pair_kernel, half),
            [shape((slots, rows, blk), bf16)] * half,
            [VMEM] * parts,
            [VMEM] * half,
            [],
        )(*even, *crossed)
        terms = [paired[0]] + [swap(paired[j], 2 * j, parts) for j in range(1, half)]
    else:
        spread = partials[0].reshape(slots, parts, rows, blk).transpose(1, 0, 2, 3)
        spread = lax.all_to_all(spread, "dp", split_axis=0, concat_axis=0, tiled=True)
        terms = [jnp.sum(spread.astype(f32), axis=0)]

    owner_grads = call(
        functools.partial(total_kernel, (n, bs, len(terms))),
        [shape((bs, rows, blk), bf16)] * n,
        [SMEM] + [VMEM] * len(terms),
        [VMEM] * n,
        [pltpu.VMEM((slots, rows, blk), bf16)],
    )(here, *terms)
    arrived = [owner_grads[0]] + [shift(owner_grads[s], s, n) for s in range(1, n)]

    first_new, second_new, weight_share = call(
        functools.partial(
            adam_kernel, (n, per, bs, pad, rows, 1.0 / math.sqrt(tok * parts))
        ),
        [shape((per, shard), f32)] * 2 + [shape((per, rows, blk), bf16)],
        [SMEM, VMEM] + [VMEM] * (2 * n),
        [VMEM] * 3,
        [
            pltpu.VMEM((slots, rows, blk), bf16),
            pltpu.VMEM((2, n * pad, shard), f32),
            pltpu.VMEM((per * rows, blk), f32),
            pltpu.VMEM((per * rows, blk), f32),
            pltpu.VMEM((per, shard), f32),
            pltpu.VMEM((per, shard), f32),
        ],
    )(table, mine, *arrived, *moments)

    if direct:
        weights_out = call(
            functools.partial(join_kernel, parts),
            shape((per, blk, blk), bf16),
            [SMEM] + [VMEM] * parts,
            VMEM,
            [],
        )(here, *plane_gather(weight_share, parts))
    else:
        weights_out = lax.all_gather(weight_share, "dp", axis=1, tiled=True)

    grad_inputs = call(
        sum_kernel, shape((tok, width // n), bf16), [VMEM] * n, VMEM, []
    )(own, *back_terms)
    return (activated, grad_inputs, weights_out, first_new, second_new)


def solution(mesh):
    in_specs = (
        P("dp", None),
        P("dp", "mp"),
        P("mp", None, None),
        P("mp", "dp"),
        P("mp", "dp"),
        P(),
        P(),
    )
    out_specs = (P("dp", "mp"), P("dp", "mp"), P("mp", None, None), P("mp", "dp"), P("mp", "dp"))
    return jax.shard_map(step, mesh=mesh, in_specs=in_specs, out_specs=out_specs, check_vma=False)
```

```python
import functools
import math

import jax
import jax.numpy as jnp
from jax import lax
from jax.experimental import pallas as pl
from jax.experimental.pallas import tpu as pltpu
from jax.sharding import PartitionSpec as P


BETA_ONE = 0.9
BETA_TWO = 0.95
LEARN_RATE = 0.01
ADAM_EPSILON = 0.05
SQRT_2_OVER_PI = math.sqrt(2.0 / math.pi)


ROOM_BYTES = 4 << 20

VMEM = pl.BlockSpec(memory_space=pltpu.VMEM)
SMEM = pl.BlockSpec(memory_space=pltpu.SMEM)
ANY = pl.BlockSpec(memory_space=pl.ANY)


def in_hbm(value):
    return pltpu.with_memory_space_constraint(value, pltpu.HBM)


def size_of(item):
    return math.prod(item.shape) * jnp.dtype(item.dtype).itemsize


def call(kernel, out_shape, in_specs, out_specs, scratch):
    def run(*args):
        outs = out_shape if isinstance(out_shape, list) else [out_shape]
        held = [x for x in scratch if hasattr(x, "shape") and x.dtype in (jnp.int32, jnp.bfloat16, jnp.float32)]
        room = sum(size_of(x) for x in (*args, *outs, *held))
        return pl.pallas_call(
            kernel,
            out_shape=out_shape,
            in_specs=in_specs,
            out_specs=out_specs,
            scratch_shapes=scratch,
            compiler_params=pltpu.CompilerParams(vmem_limit_bytes=room + ROOM_BYTES),
        )(*args)

    return run


def shape(dims, dtype):
    return jax.ShapeDtypeStruct(dims, dtype)


def paired(n):
    return n & (n - 1) == 0


def rel_to(me, other, n):
    if paired(n):
        return me ^ other
    rel = other - me
    return jnp.where(rel < 0, rel + n, rel)


def rel_from(me, other, n):
    if paired(n):
        return me ^ other
    rel = me - other
    return jnp.where(rel < 0, rel + n, rel)


def target_of(me, step, n):
    if paired(n):
        return me ^ step
    other = me + step
    return jnp.where(other >= n, other - n, other)


def target_of_static(i, step, n):
    return i ^ step if paired(n) else (i + step) % n


def which_group(value, group, count):
    found = jnp.int32(0)
    for edge in range(1, count):
        found = found + (value >= edge * group).astype(jnp.int32)
    return found


def take_rank(counts, at, live):
    rank = jnp.int32(0)
    new = []
    for i, count in enumerate(counts):
        hit = jnp.where(jnp.logical_and(live, at == i), 1, 0)
        rank = rank + hit * count
        new.append(count + hit)
    return rank, tuple(new)


def plan_kernel(cfg, here, coords, moved, table, src):
    n, per, cap, ms, bs, bw, pad = cfg
    total = n * per
    slots = n * bs
    share, grad, moment = 3 * slots, 3 * slots + per, 3 * slots + 2 * per
    out = moment + per
    spare = out + n * ms
    me = here[0]

    def fill(ref, base, size, value):
        def put(i, _):
            ref[base + i] = jnp.int32(value)
            return 0

        lax.fori_loop(0, size, put, 0, unroll=math.gcd(size, 4))

    fill(src, 0, total, -1)
    fill(table, 0, slots, -1)
    fill(table, slots, 2 * slots, 0)
    fill(table, moment, per, -1)
    fill(table, out, n * ms, 0)
    zeros = (jnp.int32(0),) * n

    for p in range(n):
        rel = rel_from(me, p, n)

        def old_slot(j, counts):
            t = moved[p * cap + j]
            live = t >= 0
            dest = which_group(t, per, n)
            k, counts = take_rank(counts, dest, live)
            src[jnp.where(live, t, total)] = rel * cap + j
            gone = jnp.logical_and(live, me == p)
            table[jnp.where(gone, out + rel_to(me, dest, n) * ms + k, spare)] = j
            came = jnp.logical_and(live, dest == me)
            table[jnp.where(came, moment + t - me * per, spare)] = rel * pad + k
            return counts

        lax.fori_loop(0, cap, old_slot, zeros, unroll=math.gcd(cap, 4))

    for w in range(n):

        def new_slot(j, counts):
            b = w * per + j
            row = coords[0, b]
            col = coords[1, b]
            source = src[b]
            band = which_group(col, bw, n)
            k, counts = take_rank(counts, band, True)
            q = w * bs + k
            near = band == me
            table[jnp.where(near, q, spare)] = source
            table[jnp.where(near, slots + q, spare)] = row
            table[jnp.where(near, 2 * slots + q, spare)] = col - me * bw
            own = me == w
            table[jnp.where(own, share + j, spare)] = source
            table[jnp.where(own, grad + j, spare)] = rel_from(me, band, n) * bs + k
            return counts

        lax.fori_loop(0, per, new_slot, zeros, unroll=math.gcd(per, 4))


def pack_kernel(cfg, table, first, second, tokens, cotangent, *rest):
    n, ms, pad, out = cfg
    packs = rest[:n]
    tokens_out, cotangent_out, first_in, second_in, sems = rest[n:]
    copies = [
        pltpu.make_async_copy(first, first_in, sems.at[0]),
        pltpu.make_async_copy(second, second_in, sems.at[1]),
        pltpu.make_async_copy(tokens, tokens_out, sems.at[2]),
        pltpu.make_async_copy(cotangent, cotangent_out, sems.at[3]),
    ]
    for copy in copies:
        copy.start()
    copies[0].wait()
    copies[1].wait()
    for s in range(n):
        for k in range(ms):
            row = table[out + s * ms + k]
            packs[s][0, k : k + 1, :] = first_in[pl.ds(row, 1), :]
            packs[s][1, k : k + 1, :] = second_in[pl.ds(row, 1), :]
        if pad > ms:
            packs[s][:, ms:pad, :] = jnp.zeros((2, pad - ms, first.shape[1]), jnp.float32)
    copies[2].wait()
    copies[3].wait()


def select_kernel(cfg, table, *rest):
    n, per, cap, bs = cfg
    shares = rest[:n]
    picked, mine, pool = rest[n:]
    slots = n * bs
    for s in range(n):
        pool[s * cap : (s + 1) * cap] = shares[s][...]

    def pick(out, base):
        def one(i, _):
            at = table[base + i]
            row = pool[jnp.maximum(at, 0)]
            out[i] = jnp.where(at >= 0, row, jnp.zeros_like(row))
            return 0

        return one

    lax.fori_loop(0, slots, pick(picked, 0), 0, unroll=4)
    lax.fori_loop(0, per, pick(mine, 3 * slots), 0, unroll=4)


def forward_kernel(cfg, here, table, tokens, cotangent, *rest):
    n, bs, bw, blk, parts = cfg
    weights_in = rest[:parts]
    rest = rest[parts:]
    activated, slopes = rest[:2]
    far = rest[2 : 1 + n]
    own = rest[1 + n]
    weights, hidden, grads = rest[2 + n :]
    slots = n * bs
    me = here[0]
    if parts == 1:
        weights = weights_in[0]
    else:
        rows = blk // parts
        d = here[1]
        for s in range(parts):
            weights[:, pl.ds(pl.multiple_of((d ^ s) * rows, rows), rows), :] = weights_in[s][...]

    def col_at(index):
        return pl.ds(pl.multiple_of(index * blk, blk), blk)

    hidden[...] = jnp.zeros_like(hidden)

    def product(w, _):
        for k in range(bs):
            q = w * bs + k
            term = jnp.dot(
                tokens[:, col_at(table[slots + q])],
                weights[q],
                preferred_element_type=jnp.float32,
            ).astype(jnp.bfloat16)
            at = col_at(table[2 * slots + q])
            hidden[:, at] = hidden[:, at] + term.astype(jnp.float32)
        return 0

    lax.fori_loop(0, n, product, 0)

    def pointwise(c, _):
        at = col_at(c)
        v = hidden[:, at]
        square = v * v
        t = jnp.tanh(v * (SQRT_2_OVER_PI + (SQRT_2_OVER_PI * 0.044715) * square))
        half = 0.5 + 0.5 * t
        value = v * half
        activated[:, at] = value.astype(jnp.bfloat16)
        slope = half + value * (1.0 - half) * (
            2.0 * SQRT_2_OVER_PI + (6.0 * 0.044715 * SQRT_2_OVER_PI) * square
        )
        slopes[:, at] = (cotangent[:, at].astype(jnp.float32) * slope).astype(jnp.bfloat16)
        return 0

    lax.fori_loop(0, bw, pointwise, 0)
    grads[...] = jnp.zeros_like(grads)

    def back(w, _):
        for k in range(bs):
            q = w * bs + k
            term = lax.dot_general(
                slopes[:, col_at(table[2 * slots + q])],
                weights[q],
                (((1,), (1,)), ((), ())),
                preferred_element_type=jnp.float32,
            )
            at = col_at(table[slots + q])
            grads[:, at] = grads[:, at] + term
        return 0

    lax.fori_loop(0, n, back, 0)
    width = own.shape[1]

    def band_of(s):
        band = target_of(me, s, n)
        return grads[:, pl.ds(pl.multiple_of(band * width, blk), width)]

    own[...] = band_of(0)
    for s in range(1, n):
        far[s - 1][...] = band_of(s).astype(jnp.bfloat16)


def grad_kernel(cfg, here, table, tokens, slopes, *rest):
    n, bs, blk, parts = cfg
    outs = rest[:parts]
    partial = rest[parts]
    slots = n * bs

    def col_at(index):
        return pl.ds(pl.multiple_of(index * blk, blk), blk)

    target = outs[0] if parts == 1 else partial

    def one(w, _):
        for k in range(bs):
            q = w * bs + k
            target[q] = lax.dot_general(
                tokens[:, col_at(table[slots + q])],
                slopes[:, col_at(table[2 * slots + q])],
                (((0,), (0,)), ((), ())),
                preferred_element_type=jnp.float32,
            ).astype(jnp.bfloat16)
        return 0

    lax.fori_loop(0, n, one, 0)
    if parts > 1:
        rows = blk // parts
        d = here[1]
        for s in range(parts):
            outs[s][...] = partial[:, pl.ds(pl.multiple_of((d ^ s) * rows, rows), rows), :]


def pair_kernel(half, *refs):
    for j in range(half):
        total = refs[j][...].astype(jnp.float32) + refs[half + j][...].astype(jnp.float32)
        refs[2 * half + j][...] = total.astype(jnp.bfloat16)


def total_kernel(cfg, here, *rest):
    n, bs, count = cfg
    terms = rest[:count]
    outs = rest[count : count + n]
    pool = rest[count + n]
    me = here[0]
    total = terms[0][...].astype(jnp.float32)
    for term in terms[1:]:
        total = total + term[...].astype(jnp.float32)
    pool[...] = total.astype(jnp.bfloat16)
    for s in range(n):
        band = target_of(me, s, n)
        outs[s][...] = pool[pl.ds(band * bs, bs)]


def adam_kernel(cfg, table, mine, *rest):
    n, per, bs, pad, rows, scale = cfg
    grads = rest[:n]
    moments = rest[n : 2 * n]
    first_out, second_out, weight_out = rest[2 * n : 2 * n + 3]
    pool, moved, grad, weight, first, second = rest[2 * n + 3 :]
    slots = n * bs
    lanes = mine.shape[2]
    for s in range(n):
        pool[s * bs : (s + 1) * bs] = grads[s][...]
        moved[:, s * pad : (s + 1) * pad, :] = moments[s][...]

    for i in range(per):
        grad[i * rows : (i + 1) * rows, :] = (
            pool[table[3 * slots + per + i]].astype(jnp.float32) * scale
        )
        weight[i * rows : (i + 1) * rows, :] = mine[i].astype(jnp.float32)
        at = table[3 * slots + 2 * per + i]
        row = jnp.maximum(at, 0)
        old_first = moved[0, pl.ds(row, 1), :]
        old_second = moved[1, pl.ds(row, 1), :]
        first[i : i + 1, :] = jnp.where(at >= 0, old_first, jnp.zeros_like(old_first))
        second[i : i + 1, :] = jnp.where(at >= 0, old_second, jnp.zeros_like(old_second))

    for r in range(rows):
        at = slice(r * lanes, (r + 1) * lanes)
        strided = pl.ds(r, per, stride=rows)
        g = grad[strided, :]
        first_new = BETA_ONE * first[:, at] + (1.0 - BETA_ONE) * g
        second_new = BETA_TWO * second[:, at] + (1.0 - BETA_TWO) * g * g
        first_out[:, at] = first_new
        second_out[:, at] = second_new
        weight[strided, :] = weight[strided, :] - LEARN_RATE * first_new / (
            jnp.sqrt(second_new) + ADAM_EPSILON
        )
    for i in range(per):
        weight_out[i] = weight[i * rows : (i + 1) * rows, :].astype(jnp.bfloat16)


def join_kernel(parts, here, *rest):
    out = rest[parts]
    rows = rest[0].shape[1]
    d = here[1]
    for s in range(parts):
        out[:, pl.ds(pl.multiple_of((d ^ s) * rows, rows), rows), :] = rest[s][...]


def sum_kernel(own, *rest):
    total = own[...]
    for term in rest[:-1]:
        total = total + term[...].astype(jnp.float32)
    rest[-1][...] = total.astype(jnp.bfloat16)


def swap(value, bits, parts):
    return lax.ppermute(value, "dp", [(i, i ^ bits) for i in range(parts)])


def shift(value, step, n):
    return lax.ppermute(value, "mp", [(i, target_of_static(i, step, n)) for i in range(n)])


def plane_gather(value, parts):
    pieces = [value] + [None] * (parts - 1)
    for s in range(2, parts, 2):
        pieces[s] = swap(value, s, parts)
    for s in range(0, parts, 2):
        pieces[s + 1] = swap(pieces[s], 1, parts)
    return pieces


def step(tokens_in, cotangent, old_weights, old_first, old_second, new_coords, moved_to):
    n = lax.axis_size("mp")
    parts = lax.axis_size("dp")
    me = lax.axis_index("mp")
    d = lax.axis_index("dp")
    cap, blk = old_weights.shape[:2]
    total = new_coords.shape[0]
    per = total // n
    shard = old_first.shape[1]
    rows = blk // parts
    tok, width = tokens_in.shape
    bw = cotangent.shape[1] // blk
    ms = cap // n
    pad = -(-ms // 8) * 8
    bs = 2 * per // n + 1
    slots = n * bs
    direct = rows % 16 == 0 and parts & (parts - 1) == 0
    bf16, f32 = jnp.bfloat16, jnp.float32
    here = jnp.stack([me, d]).astype(jnp.int32)

    share = lax.dynamic_slice_in_dim(old_weights, d * rows, rows, 1)
    shares = [share] + [shift(share, s, n) for s in range(1, n)]

    out = 3 * slots + 3 * per
    table = call(
        functools.partial(plan_kernel, (n, per, cap, ms, bs, bw, pad)),
        shape((out + n * ms + 4,), jnp.int32),
        [SMEM] * 3,
        SMEM,
        [pltpu.SMEM((total + 8,), jnp.int32)],
    )(here, in_hbm(new_coords.T), in_hbm(moved_to))

    picked, mine = call(
        functools.partial(select_kernel, (n, per, cap, bs)),
        [shape((slots, rows, blk), bf16), shape((per, rows, blk), bf16)],
        [SMEM] + [VMEM] * n,
        [VMEM, VMEM],
        [pltpu.VMEM((n * cap, rows, blk), bf16)],
    )(table, *shares)

    if direct:
        pieces = plane_gather(picked, parts)
    else:
        gathered = lax.all_gather(picked, "dp", axis=0)
        pieces = [gathered.transpose(1, 0, 2, 3).reshape(slots, blk, blk)]

    packed = call(
        functools.partial(pack_kernel, (n, ms, pad, out)),
        [shape((2, pad, shard), f32)] * n
        + [shape(tokens_in.shape, bf16), shape(cotangent.shape, bf16)],
        [SMEM] + [ANY] * 4,
        [VMEM] * (n + 2),
        [
            pltpu.VMEM(old_first.shape, f32),
            pltpu.VMEM(old_second.shape, f32),
            pltpu.SemaphoreType.DMA((4,)),
        ],
    )(table, *[in_hbm(x) for x in (old_first, old_second, tokens_in, cotangent)])
    packs = packed[:n]
    tokens, cotangents = packed[n:]
    moments = [packs[0]] + [shift(packs[s], s, n) for s in range(1, n)]

    results = call(
        functools.partial(forward_kernel, (n, bs, bw, blk, len(pieces))),
        [shape((tok, bw * blk), bf16)] * 2
        + [shape((tok, width // n), bf16)] * (n - 1)
        + [shape((tok, width // n), f32)],
        [SMEM, SMEM, VMEM, VMEM] + [VMEM] * len(pieces),
        [VMEM] * (n + 2),
        [
            pltpu.VMEM((slots, blk, blk), bf16),
            pltpu.VMEM((tok, bw * blk), f32),
            pltpu.VMEM((tok, width), f32),
        ],
    )(here, table, tokens, cotangents, *pieces)
    activated, slopes = results[:2]
    far, own = results[2 : 1 + n], results[1 + n]
    back_terms = [shift(far[s - 1], s, n) for s in range(1, n)]

    count = parts if direct else 1
    partials = call(
        functools.partial(grad_kernel, (n, bs, blk, count)),
        [shape((slots, blk // count, blk), bf16)] * count,
        [SMEM, SMEM, VMEM, VMEM],
        [VMEM] * count,
        [pltpu.VMEM((slots, blk, blk), bf16)],
    )(here, table, tokens, slopes)

    if direct:
        half = parts // 2
        even = [partials[2 * j] for j in range(half)]
        crossed = [swap(partials[2 * j + 1], 1, parts) for j in range(half)]
        paired = call(
            functools.partial(pair_kernel, half),
            [shape((slots, rows, blk), bf16)] * half,
            [VMEM] * parts,
            [VMEM] * half,
            [],
        )(*even, *crossed)
        terms = [paired[0]] + [swap(paired[j], 2 * j, parts) for j in range(1, half)]
    else:
        spread = partials[0].reshape(slots, parts, rows, blk).transpose(1, 0, 2, 3)
        spread = lax.all_to_all(spread, "dp", split_axis=0, concat_axis=0, tiled=True)
        terms = [jnp.sum(spread.astype(f32), axis=0)]

    owner_grads = call(
        functools.partial(total_kernel, (n, bs, len(terms))),
        [shape((bs, rows, blk), bf16)] * n,
        [SMEM] + [VMEM] * len(terms),
        [VMEM] * n,
        [pltpu.VMEM((slots, rows, blk), bf16)],
    )(here, *terms)
    arrived = [owner_grads[0]] + [shift(owner_grads[s], s, n) for s in range(1, n)]

    first_new, second_new, weight_share = call(
        functools.partial(
            adam_kernel, (n, per, bs, pad, rows, 1.0 / math.sqrt(tok * parts))
        ),
        [shape((per, shard), f32)] * 2 + [shape((per, rows, blk), bf16)],
        [SMEM, VMEM] + [VMEM] * (2 * n),
        [VMEM] * 3,
        [
            pltpu.VMEM((slots, rows, blk), bf16),
            pltpu.VMEM((2, n * pad, shard), f32),
            pltpu.VMEM((per * rows, blk), f32),
            pltpu.VMEM((per * rows, blk), f32),
            pltpu.VMEM((per, shard), f32),
            pltpu.VMEM((per, shard), f32),
        ],
    )(table, mine, *arrived, *moments)

    if direct:
        weights_out = call(
            functools.partial(join_kernel, parts),
            shape((per, blk, blk), bf16),
            [SMEM] + [VMEM] * parts,
            VMEM,
            [],
        )(here, *plane_gather(weight_share, parts))
    else:
        weights_out = lax.all_gather(weight_share, "dp", axis=1, tiled=True)

    grad_inputs = call(
        sum_kernel, shape((tok, width // n), bf16), [VMEM] * n, VMEM, []
    )(own, *back_terms)
    return (activated, grad_inputs, weights_out, first_new, second_new)


def solution(mesh):
    in_specs = (
        P("dp", None),
        P("dp", "mp"),
        P("mp", None, None),
        P("mp", "dp"),
        P("mp", "dp"),
        P(),
        P(),
    )
    out_specs = (P("dp", "mp"), P("dp", "mp"), P("mp", None, None), P("mp", "dp"), P("mp", "dp"))
    return jax.shard_map(step, mesh=mesh, in_specs=in_specs, out_specs=out_specs, check_vma=False)
```

```python
import functools
import math

import jax
import jax.numpy as jnp
from jax import lax
from jax.experimental import pallas as pl
from jax.experimental.pallas import tpu as pltpu
from jax.sharding import PartitionSpec as P


BETA_ONE = 0.9
BETA_TWO = 0.95
LEARN_RATE = 0.01
ADAM_EPSILON = 0.05
SQRT_2_OVER_PI = math.sqrt(2.0 / math.pi)


ROOM_BYTES = 4 << 20

VMEM = pl.BlockSpec(memory_space=pltpu.VMEM)
SMEM = pl.BlockSpec(memory_space=pltpu.SMEM)
ANY = pl.BlockSpec(memory_space=pl.ANY)


def in_hbm(value):
    return pltpu.with_memory_space_constraint(value, pltpu.HBM)


def size_of(item):
    return math.prod(item.shape) * jnp.dtype(item.dtype).itemsize


def call(kernel, out_shape, in_specs, out_specs, scratch):
    def run(*args):
        outs = out_shape if isinstance(out_shape, list) else [out_shape]
        held = [x for x in scratch if hasattr(x, "shape") and x.dtype in (jnp.int32, jnp.bfloat16, jnp.float32)]
        room = sum(size_of(x) for x in (*args, *outs, *held))
        return pl.pallas_call(
            kernel,
            out_shape=out_shape,
            in_specs=in_specs,
            out_specs=out_specs,
            scratch_shapes=scratch,
            compiler_params=pltpu.CompilerParams(vmem_limit_bytes=room + ROOM_BYTES),
        )(*args)

    return run


def shape(dims, dtype):
    return jax.ShapeDtypeStruct(dims, dtype)


def paired(n):
    return n & (n - 1) == 0


def rel_to(me, other, n):
    if paired(n):
        return me ^ other
    rel = other - me
    return jnp.where(rel < 0, rel + n, rel)


def rel_from(me, other, n):
    if paired(n):
        return me ^ other
    rel = me - other
    return jnp.where(rel < 0, rel + n, rel)


def target_of(me, step, n):
    if paired(n):
        return me ^ step
    other = me + step
    return jnp.where(other >= n, other - n, other)


def target_of_static(i, step, n):
    return i ^ step if paired(n) else (i + step) % n


def which_group(value, group, count):
    found = jnp.int32(0)
    for edge in range(1, count):
        found = found + (value >= edge * group).astype(jnp.int32)
    return found


def take_rank(counts, at, live):
    rank = jnp.int32(0)
    new = []
    for i, count in enumerate(counts):
        hit = jnp.where(jnp.logical_and(live, at == i), 1, 0)
        rank = rank + hit * count
        new.append(count + hit)
    return rank, tuple(new)


def plan_kernel(cfg, here, coords, moved, table, src):
    n, per, cap, ms, bs, bw, pad = cfg
    total = n * per
    slots = n * bs
    share, grad, moment = 3 * slots, 3 * slots + per, 3 * slots + 2 * per
    out = moment + per
    spare = out + n * ms
    me = here[0]

    def fill(ref, base, size, value):
        def put(i, _):
            ref[base + i] = jnp.int32(value)
            return 0

        lax.fori_loop(0, size, put, 0, unroll=math.gcd(size, 4))

    fill(src, 0, total, -1)
    fill(table, 0, slots, -1)
    fill(table, slots, 2 * slots, 0)
    fill(table, moment, per, -1)
    fill(table, out, n * ms, 0)
    zeros = (jnp.int32(0),) * n

    for p in range(n):
        rel = rel_from(me, p, n)

        def old_slot(j, counts):
            t = moved[p * cap + j]
            live = t >= 0
            dest = which_group(t, per, n)
            k, counts = take_rank(counts, dest, live)
            src[jnp.where(live, t, total)] = rel * cap + j
            gone = jnp.logical_and(live, me == p)
            table[jnp.where(gone, out + rel_to(me, dest, n) * ms + k, spare)] = j
            came = jnp.logical_and(live, dest == me)
            table[jnp.where(came, moment + t - me * per, spare)] = rel * pad + k
            return counts

        lax.fori_loop(0, cap, old_slot, zeros, unroll=math.gcd(cap, 4))

    for w in range(n):

        def new_slot(j, counts):
            b = w * per + j
            row = coords[0, b]
            col = coords[1, b]
            source = src[b]
            band = which_group(col, bw, n)
            k, counts = take_rank(counts, band, True)
            q = w * bs + k
            near = band == me
            table[jnp.where(near, q, spare)] = source
            table[jnp.where(near, slots + q, spare)] = row
            table[jnp.where(near, 2 * slots + q, spare)] = col - me * bw
            own = me == w
            table[jnp.where(own, share + j, spare)] = source
            table[jnp.where(own, grad + j, spare)] = rel_from(me, band, n) * bs + k
            return counts

        lax.fori_loop(0, per, new_slot, zeros, unroll=math.gcd(per, 4))


def pack_kernel(cfg, table, first, second, tokens, cotangent, *rest):
    n, ms, pad, out = cfg
    packs = rest[:n]
    tokens_out, cotangent_out, first_in, second_in, sems = rest[n:]
    copies = [
        pltpu.make_async_copy(first, first_in, sems.at[0]),
        pltpu.make_async_copy(second, second_in, sems.at[1]),
        pltpu.make_async_copy(tokens, tokens_out, sems.at[2]),
        pltpu.make_async_copy(cotangent, cotangent_out, sems.at[3]),
    ]
    for copy in copies:
        copy.start()
    copies[0].wait()
    copies[1].wait()
    for s in range(n):
        for k in range(ms):
            row = table[out + s * ms + k]
            packs[s][0, k : k + 1, :] = first_in[pl.ds(row, 1), :]
            packs[s][1, k : k + 1, :] = second_in[pl.ds(row, 1), :]
        if pad > ms:
            packs[s][:, ms:pad, :] = jnp.zeros((2, pad - ms, first.shape[1]), jnp.float32)
    copies[2].wait()
    copies[3].wait()


def select_kernel(cfg, table, *rest):
    n, per, cap, bs = cfg
    shares = rest[:n]
    picked, mine, pool = rest[n:]
    slots = n * bs
    for s in range(n):
        pool[s * cap : (s + 1) * cap] = shares[s][...]

    def pick(out, base):
        def one(i, _):
            at = table[base + i]
            row = pool[jnp.maximum(at, 0)]
            out[i] = jnp.where(at >= 0, row, jnp.zeros_like(row))
            return 0

        return one

    lax.fori_loop(0, slots, pick(picked, 0), 0, unroll=4)
    lax.fori_loop(0, per, pick(mine, 3 * slots), 0, unroll=4)


def forward_kernel(cfg, here, table, tokens, cotangent, *rest):
    n, bs, bw, blk, parts = cfg
    weights_in = rest[:parts]
    rest = rest[parts:]
    activated, slopes = rest[:2]
    odd, near, even = split_steps(n)
    relay = rest[2] if odd else None
    at = 2 + (1 if odd else 0)
    nears = rest[at : at + len(near)]
    at += len(near)
    evens = rest[at : at + len(even)]
    own, weights, hidden, grads = rest[at + len(even) :]
    slots = n * bs
    me = here[0]
    if parts == 1:
        weights = weights_in[0]
    else:
        rows = blk // parts
        d = here[1]
        for s in range(parts):
            weights[:, pl.ds(pl.multiple_of((d ^ s) * rows, rows), rows), :] = weights_in[s][...]

    def col_at(index):
        return pl.ds(pl.multiple_of(index * blk, blk), blk)

    hidden[...] = jnp.zeros_like(hidden)

    def product(w, _):
        for k in range(bs):
            q = w * bs + k
            term = jnp.dot(
                tokens[:, col_at(table[slots + q])],
                weights[q],
                preferred_element_type=jnp.float32,
            ).astype(jnp.bfloat16)
            at = col_at(table[2 * slots + q])
            hidden[:, at] = hidden[:, at] + term.astype(jnp.float32)
        return 0

    lax.fori_loop(0, n, product, 0)

    def pointwise(c, _):
        at = col_at(c)
        v = hidden[:, at]
        square = v * v
        t = jnp.tanh(v * (SQRT_2_OVER_PI + (SQRT_2_OVER_PI * 0.044715) * square))
        half = 0.5 + 0.5 * t
        value = v * half
        activated[:, at] = value.astype(jnp.bfloat16)
        slope = half + value * (1.0 - half) * (
            2.0 * SQRT_2_OVER_PI + (6.0 * 0.044715 * SQRT_2_OVER_PI) * square
        )
        slopes[:, at] = (cotangent[:, at].astype(jnp.float32) * slope).astype(jnp.bfloat16)
        return 0

    lax.fori_loop(0, bw, pointwise, 0)
    grads[...] = jnp.zeros_like(grads)

    def back(w, _):
        for k in range(bs):
            q = w * bs + k
            term = lax.dot_general(
                slopes[:, col_at(table[2 * slots + q])],
                weights[q],
                (((1,), (1,)), ((), ())),
                preferred_element_type=jnp.float32,
            )
            at = col_at(table[slots + q])
            grads[:, at] = grads[:, at] + term
        return 0

    lax.fori_loop(0, n, back, 0)
    width = own.shape[1]

    def band_of(s):
        band = target_of(me, s, n)
        return grads[:, pl.ds(pl.multiple_of(band * width, blk), width)]

    own[...] = band_of(0)
    for i, s in enumerate(odd):
        relay[i] = band_of(s).astype(jnp.bfloat16)
    for i, s in enumerate(near):
        nears[i][...] = band_of(s).astype(jnp.bfloat16)
    for i, s in enumerate(even):
        evens[i][...] = band_of(s)


def grad_kernel(cfg, here, table, tokens, slopes, *rest):
    n, bs, blk, parts = cfg
    outs = rest[:parts]
    partial = rest[parts]
    slots = n * bs

    def col_at(index):
        return pl.ds(pl.multiple_of(index * blk, blk), blk)

    target = outs[0] if parts == 1 else partial

    def one(w, _):
        for k in range(bs):
            q = w * bs + k
            target[q] = lax.dot_general(
                tokens[:, col_at(table[slots + q])],
                slopes[:, col_at(table[2 * slots + q])],
                (((0,), (0,)), ((), ())),
                preferred_element_type=jnp.float32,
            ).astype(jnp.bfloat16)
        return 0

    lax.fori_loop(0, n, one, 0)
    if parts > 1:
        rows = blk // parts
        d = here[1]
        for s in range(parts):
            outs[s][...] = partial[:, pl.ds(pl.multiple_of((d ^ s) * rows, rows), rows), :]


def pair_kernel(half, *refs):
    for j in range(half):
        total = refs[j][...].astype(jnp.float32) + refs[half + j][...].astype(jnp.float32)
        refs[2 * half + j][...] = total.astype(jnp.bfloat16)


def total_kernel(cfg, here, *rest):
    n, bs, count = cfg
    terms = rest[:count]
    outs = rest[count : count + n]
    pool = rest[count + n]
    me = here[0]
    total = terms[0][...].astype(jnp.float32)
    for term in terms[1:]:
        total = total + term[...].astype(jnp.float32)
    pool[...] = total.astype(jnp.bfloat16)
    for s in range(n):
        band = target_of(me, s, n)
        outs[s][...] = pool[pl.ds(band * bs, bs)]


def adam_kernel(cfg, table, mine, *rest):
    n, per, bs, pad, rows, scale = cfg
    grads = rest[:n]
    moments = rest[n : 2 * n]
    first_out, second_out, weight_out = rest[2 * n : 2 * n + 3]
    pool, moved, grad, weight, first, second = rest[2 * n + 3 :]
    slots = n * bs
    lanes = mine.shape[2]
    for s in range(n):
        pool[s * bs : (s + 1) * bs] = grads[s][...]
        moved[:, s * pad : (s + 1) * pad, :] = moments[s][...]

    for i in range(per):
        grad[i * rows : (i + 1) * rows, :] = (
            pool[table[3 * slots + per + i]].astype(jnp.float32) * scale
        )
        weight[i * rows : (i + 1) * rows, :] = mine[i].astype(jnp.float32)
        at = table[3 * slots + 2 * per + i]
        row = jnp.maximum(at, 0)
        old_first = moved[0, pl.ds(row, 1), :]
        old_second = moved[1, pl.ds(row, 1), :]
        first[i : i + 1, :] = jnp.where(at >= 0, old_first, jnp.zeros_like(old_first))
        second[i : i + 1, :] = jnp.where(at >= 0, old_second, jnp.zeros_like(old_second))

    for r in range(rows):
        at = slice(r * lanes, (r + 1) * lanes)
        strided = pl.ds(r, per, stride=rows)
        g = grad[strided, :]
        first_new = BETA_ONE * first[:, at] + (1.0 - BETA_ONE) * g
        second_new = BETA_TWO * second[:, at] + (1.0 - BETA_TWO) * g * g
        first_out[:, at] = first_new
        second_out[:, at] = second_new
        weight[strided, :] = weight[strided, :] - LEARN_RATE * first_new / (
            jnp.sqrt(second_new) + ADAM_EPSILON
        )
    for i in range(per):
        weight_out[i] = weight[i * rows : (i + 1) * rows, :].astype(jnp.bfloat16)


def join_kernel(parts, here, *rest):
    out = rest[parts]
    rows = rest[0].shape[1]
    d = here[1]
    for s in range(parts):
        out[:, pl.ds(pl.multiple_of((d ^ s) * rows, rows), rows), :] = rest[s][...]


def split_steps(n):
    steps = list(range(1, n))
    if not paired(n):
        return [], [], steps
    return steps[2::2], steps[:1], steps[1::2]


def relay_kernel(count, *refs):
    evens, outs = refs[:count], refs[-2 * count :]
    half = evens[0].shape[0] // 2
    for i in range(count):
        total = evens[i][...]
        if len(refs) > 3 * count:
            total = total + refs[count][i].astype(jnp.float32)
        total = total.astype(jnp.bfloat16)
        outs[2 * i][...] = total[:half]
        outs[2 * i + 1][...] = total[half:]


def sum_kernel(cfg, own, *rest):
    evens, nears = cfg
    out = rest[-1]
    half = own.shape[0] // 2
    for h in range(2):
        rows = slice(h * half, (h + 1) * half)
        total = own[rows]
        for i in range(evens):
            total = total + rest[2 * i + h][...].astype(jnp.float32)
        for i in range(nears):
            total = total + rest[2 * evens + i][rows].astype(jnp.float32)
        out[rows] = total.astype(jnp.bfloat16)


def swap(value, bits, parts):
    return lax.ppermute(value, "dp", [(i, i ^ bits) for i in range(parts)])


def shift(value, step, n):
    return lax.ppermute(value, "mp", [(i, target_of_static(i, step, n)) for i in range(n)])


def plane_gather(value, parts):
    pieces = [value] + [None] * (parts - 1)
    for s in range(2, parts, 2):
        pieces[s] = swap(value, s, parts)
    for s in range(0, parts, 2):
        pieces[s + 1] = swap(pieces[s], 1, parts)
    return pieces


def step(tokens_in, cotangent, old_weights, old_first, old_second, new_coords, moved_to):
    n = lax.axis_size("mp")
    parts = lax.axis_size("dp")
    me = lax.axis_index("mp")
    d = lax.axis_index("dp")
    cap, blk = old_weights.shape[:2]
    total = new_coords.shape[0]
    per = total // n
    shard = old_first.shape[1]
    rows = blk // parts
    tok, width = tokens_in.shape
    bw = cotangent.shape[1] // blk
    ms = cap // n
    pad = -(-ms // 8) * 8
    bs = 2 * per // n + 1
    slots = n * bs
    direct = rows % 16 == 0 and parts & (parts - 1) == 0
    bf16, f32 = jnp.bfloat16, jnp.float32
    here = jnp.stack([me, d]).astype(jnp.int32)

    share = lax.dynamic_slice_in_dim(old_weights, d * rows, rows, 1)
    shares = [share] + [shift(share, s, n) for s in range(1, n)]

    out = 3 * slots + 3 * per
    table = call(
        functools.partial(plan_kernel, (n, per, cap, ms, bs, bw, pad)),
        shape((out + n * ms + 4,), jnp.int32),
        [SMEM] * 3,
        SMEM,
        [pltpu.SMEM((total + 8,), jnp.int32)],
    )(here, in_hbm(new_coords.T), in_hbm(moved_to))

    picked, mine = call(
        functools.partial(select_kernel, (n, per, cap, bs)),
        [shape((slots, rows, blk), bf16), shape((per, rows, blk), bf16)],
        [SMEM] + [VMEM] * n,
        [VMEM, VMEM],
        [pltpu.VMEM((n * cap, rows, blk), bf16)],
    )(table, *shares)

    if direct:
        pieces = plane_gather(picked, parts)
    else:
        gathered = lax.all_gather(picked, "dp", axis=0)
        pieces = [gathered.transpose(1, 0, 2, 3).reshape(slots, blk, blk)]

    packed = call(
        functools.partial(pack_kernel, (n, ms, pad, out)),
        [shape((2, pad, shard), f32)] * n
        + [shape(tokens_in.shape, bf16), shape(cotangent.shape, bf16)],
        [SMEM] + [ANY] * 4,
        [VMEM] * (n + 2),
        [
            pltpu.VMEM(old_first.shape, f32),
            pltpu.VMEM(old_second.shape, f32),
            pltpu.SemaphoreType.DMA((4,)),
        ],
    )(table, *[in_hbm(x) for x in (old_first, old_second, tokens_in, cotangent)])
    packs = packed[:n]
    tokens, cotangents = packed[n:]
    moments = [packs[0]] + [shift(packs[s], s, n) for s in range(1, n)]

    odd, near, even = split_steps(n)
    results = call(
        functools.partial(forward_kernel, (n, bs, bw, blk, len(pieces))),
        [shape((tok, bw * blk), bf16)] * 2
        + [shape((len(odd), tok, width // n), bf16)] * min(len(odd), 1)
        + [shape((tok, width // n), bf16)] * len(near)
        + [shape((tok, width // n), f32)] * (len(even) + 1),
        [SMEM, SMEM, VMEM, VMEM] + [VMEM] * len(pieces),
        [VMEM] * (3 + min(len(odd), 1) + len(near) + len(even)),
        [
            pltpu.VMEM((slots, blk, blk), bf16),
            pltpu.VMEM((tok, bw * blk), f32),
            pltpu.VMEM((tok, width), f32),
        ],
    )(here, table, tokens, cotangents, *pieces)
    activated, slopes = results[:2]
    rest = list(results[2:])
    relayed = [shift(rest.pop(0), 1, n)] if odd else []
    nears = [rest.pop(0) for _ in near]
    evens, own = rest[:-1], rest[-1]

    count = parts if direct else 1
    partials = call(
        functools.partial(grad_kernel, (n, bs, blk, count)),
        [shape((slots, blk // count, blk), bf16)] * count,
        [SMEM, SMEM, VMEM, VMEM],
        [VMEM] * count,
        [pltpu.VMEM((slots, blk, blk), bf16)],
    )(here, table, tokens, slopes)

    halves = call(
        functools.partial(relay_kernel, len(even)),
        [shape((tok // 2, width // n), bf16)] * (2 * len(even)),
        [VMEM] * (len(even) + len(relayed)),
        [VMEM] * (2 * len(even)),
        [],
    )(*evens, *relayed)
    back_terms = []
    for i, s in enumerate(even):
        back_terms += [shift(halves[2 * i + h], s, n) for h in range(2)]
    back_terms += [shift(x, s, n) for x, s in zip(nears, near)]

    if direct:
        half = parts // 2
        kept = [partials[2 * j] for j in range(half)]
        crossed = [swap(partials[2 * j + 1], 1, parts) for j in range(half)]
        summed = call(
            functools.partial(pair_kernel, half),
            [shape((slots, rows, blk), bf16)] * half,
            [VMEM] * parts,
            [VMEM] * half,
            [],
        )(*kept, *crossed)
        terms = [summed[0]] + [swap(summed[j], 2 * j, parts) for j in range(1, half)]
    else:
        spread = partials[0].reshape(slots, parts, rows, blk).transpose(1, 0, 2, 3)
        spread = lax.all_to_all(spread, "dp", split_axis=0, concat_axis=0, tiled=True)
        terms = [jnp.sum(spread.astype(f32), axis=0)]

    owner_grads = call(
        functools.partial(total_kernel, (n, bs, len(terms))),
        [shape((bs, rows, blk), bf16)] * n,
        [SMEM] + [VMEM] * len(terms),
        [VMEM] * n,
        [pltpu.VMEM((slots, rows, blk), bf16)],
    )(here, *terms)
    arrived = [owner_grads[0]] + [shift(owner_grads[s], s, n) for s in range(1, n)]

    first_new, second_new, weight_share = call(
        functools.partial(
            adam_kernel, (n, per, bs, pad, rows, 1.0 / math.sqrt(tok * parts))
        ),
        [shape((per, shard), f32)] * 2 + [shape((per, rows, blk), bf16)],
        [SMEM, VMEM] + [VMEM] * (2 * n),
        [VMEM] * 3,
        [
            pltpu.VMEM((slots, rows, blk), bf16),
            pltpu.VMEM((2, n * pad, shard), f32),
            pltpu.VMEM((per * rows, blk), f32),
            pltpu.VMEM((per * rows, blk), f32),
            pltpu.VMEM((per, shard), f32),
            pltpu.VMEM((per, shard), f32),
        ],
    )(table, mine, *arrived, *moments)

    if direct:
        weights_out = call(
            functools.partial(join_kernel, parts),
            shape((per, blk, blk), bf16),
            [SMEM] + [VMEM] * parts,
            VMEM,
            [],
        )(here, *plane_gather(weight_share, parts))
    else:
        weights_out = lax.all_gather(weight_share, "dp", axis=1, tiled=True)

    grad_inputs = call(
        functools.partial(sum_kernel, (len(even), len(near))),
        shape((tok, width // n), bf16),
        [VMEM] * (1 + len(back_terms)),
        VMEM,
        [],
    )(own, *back_terms)
    return (activated, grad_inputs, weights_out, first_new, second_new)


def solution(mesh):
    in_specs = (
        P("dp", None),
        P("dp", "mp"),
        P("mp", None, None),
        P("mp", "dp"),
        P("mp", "dp"),
        P(),
        P(),
    )
    out_specs = (P("dp", "mp"), P("dp", "mp"), P("mp", None, None), P("mp", "dp"), P("mp", "dp"))
    return jax.shard_map(step, mesh=mesh, in_specs=in_specs, out_specs=out_specs, check_vma=False)
```

```python
import functools
import math

import jax
import jax.numpy as jnp
from jax import lax
from jax.experimental import pallas as pl
from jax.experimental.pallas import tpu as pltpu
from jax.sharding import PartitionSpec as P


BETA_ONE = 0.9
BETA_TWO = 0.95
LEARN_RATE = 0.01
ADAM_EPSILON = 0.05
SQRT_2_OVER_PI = math.sqrt(2.0 / math.pi)


ROOM_BYTES = 4 << 20

VMEM = pl.BlockSpec(memory_space=pltpu.VMEM)
SMEM = pl.BlockSpec(memory_space=pltpu.SMEM)
ANY = pl.BlockSpec(memory_space=pl.ANY)


def in_hbm(value):
    return pltpu.with_memory_space_constraint(value, pltpu.HBM)


def size_of(item):
    return math.prod(item.shape) * jnp.dtype(item.dtype).itemsize


def call(kernel, out_shape, in_specs, out_specs, scratch):
    def run(*args):
        outs = out_shape if isinstance(out_shape, list) else [out_shape]
        held = [x for x in scratch if hasattr(x, "shape") and x.dtype in (jnp.int32, jnp.bfloat16, jnp.float32)]
        room = sum(size_of(x) for x in (*args, *outs, *held))
        return pl.pallas_call(
            kernel,
            out_shape=out_shape,
            in_specs=in_specs,
            out_specs=out_specs,
            scratch_shapes=scratch,
            compiler_params=pltpu.CompilerParams(vmem_limit_bytes=room + ROOM_BYTES),
        )(*args)

    return run


def shape(dims, dtype):
    return jax.ShapeDtypeStruct(dims, dtype)


def paired(n):
    return n & (n - 1) == 0


def rel_to(me, other, n):
    if paired(n):
        return me ^ other
    rel = other - me
    return jnp.where(rel < 0, rel + n, rel)


def rel_from(me, other, n):
    if paired(n):
        return me ^ other
    rel = me - other
    return jnp.where(rel < 0, rel + n, rel)


def target_of(me, step, n):
    if paired(n):
        return me ^ step
    other = me + step
    return jnp.where(other >= n, other - n, other)


def target_of_static(i, step, n):
    return i ^ step if paired(n) else (i + step) % n


def which_group(value, group, count):
    found = jnp.int32(0)
    for edge in range(1, count):
        found = found + (value >= edge * group).astype(jnp.int32)
    return found


def take_rank(counts, at, live):
    rank = jnp.int32(0)
    new = []
    for i, count in enumerate(counts):
        hit = jnp.where(jnp.logical_and(live, at == i), 1, 0)
        rank = rank + hit * count
        new.append(count + hit)
    return rank, tuple(new)


def plan_kernel(cfg, here, coords, moved, table, src):
    n, per, cap, ms, bs, bw, pad = cfg
    total = n * per
    slots = n * bs
    share, grad, moment = 3 * slots, 3 * slots + per, 3 * slots + 2 * per
    out = moment + per
    spare = out + n * ms
    me = here[0]

    def fill(ref, base, size, value):
        def put(i, _):
            ref[base + i] = jnp.int32(value)
            return 0

        lax.fori_loop(0, size, put, 0, unroll=math.gcd(size, 4))

    fill(src, 0, total, -1)
    fill(table, 0, slots, -1)
    fill(table, slots, 2 * slots, 0)
    fill(table, moment, per, -1)
    fill(table, out, n * ms, 0)
    zeros = (jnp.int32(0),) * n

    for p in range(n):
        rel = rel_from(me, p, n)

        def old_slot(j, counts):
            t = moved[p * cap + j]
            live = t >= 0
            dest = which_group(t, per, n)
            k, counts = take_rank(counts, dest, live)
            src[jnp.where(live, t, total)] = rel * cap + j
            gone = jnp.logical_and(live, me == p)
            table[jnp.where(gone, out + rel_to(me, dest, n) * ms + k, spare)] = j
            came = jnp.logical_and(live, dest == me)
            table[jnp.where(came, moment + t - me * per, spare)] = rel * pad + k
            return counts

        lax.fori_loop(0, cap, old_slot, zeros, unroll=math.gcd(cap, 4))

    for w in range(n):

        def new_slot(j, counts):
            b = w * per + j
            row = coords[0, b]
            col = coords[1, b]
            source = src[b]
            band = which_group(col, bw, n)
            k, counts = take_rank(counts, band, True)
            q = w * bs + k
            near = band == me
            table[jnp.where(near, q, spare)] = source
            table[jnp.where(near, slots + q, spare)] = row
            table[jnp.where(near, 2 * slots + q, spare)] = col - me * bw
            own = me == w
            table[jnp.where(own, share + j, spare)] = source
            table[jnp.where(own, grad + j, spare)] = rel_from(me, band, n) * bs + k
            return counts

        lax.fori_loop(0, per, new_slot, zeros, unroll=math.gcd(per, 4))


def pack_kernel(cfg, table, first, second, tokens, cotangent, *rest):
    n, ms, pad, out = cfg
    packs = rest[:n]
    tokens_out, cotangent_out, first_in, second_in, sems = rest[n:]
    copies = [
        pltpu.make_async_copy(first, first_in, sems.at[0]),
        pltpu.make_async_copy(second, second_in, sems.at[1]),
        pltpu.make_async_copy(tokens, tokens_out, sems.at[2]),
        pltpu.make_async_copy(cotangent, cotangent_out, sems.at[3]),
    ]
    for copy in copies:
        copy.start()
    copies[0].wait()
    copies[1].wait()
    for s in range(n):
        for k in range(ms):
            row = table[out + s * ms + k]
            packs[s][0, k : k + 1, :] = first_in[pl.ds(row, 1), :]
            packs[s][1, k : k + 1, :] = second_in[pl.ds(row, 1), :]
        if pad > ms:
            packs[s][:, ms:pad, :] = jnp.zeros((2, pad - ms, first.shape[1]), jnp.float32)
    copies[2].wait()
    copies[3].wait()


def share_kernel(weights, out, sem):
    rows = out.shape[1]
    at = pl.multiple_of(lax.axis_index("dp") * rows, rows)
    copy = pltpu.make_async_copy(weights.at[:, pl.ds(at, rows), :], out, sem)
    copy.start()
    copy.wait()


def select_kernel(cfg, table, *rest):
    n, per, cap, bs = cfg
    shares = rest[:n]
    picked, mine, pool = rest[n:]
    slots = n * bs
    for s in range(n):
        pool[s * cap : (s + 1) * cap] = shares[s][...]

    def pick(out, base):
        def one(i, _):
            at = table[base + i]
            row = pool[jnp.maximum(at, 0)]
            out[i] = jnp.where(at >= 0, row, jnp.zeros_like(row))
            return 0

        return one

    lax.fori_loop(0, slots, pick(picked, 0), 0, unroll=4)
    lax.fori_loop(0, per, pick(mine, 3 * slots), 0, unroll=4)


def forward_kernel(cfg, here, table, tokens, cotangent, *rest):
    n, bs, bw, blk, parts = cfg
    weights_in = rest[:parts]
    rest = rest[parts:]
    activated, slopes = rest[:2]
    odd, near, even = split_steps(n)
    relay = rest[2] if odd else None
    at = 2 + (1 if odd else 0)
    nears = rest[at : at + len(near)]
    at += len(near)
    evens = rest[at : at + len(even)]
    own, weights, hidden, grads = rest[at + len(even) :]
    slots = n * bs
    me = here[0]
    if parts == 1:
        weights = weights_in[0]
    else:
        rows = blk // parts
        d = here[1]
        for s in range(parts):
            weights[:, pl.ds(pl.multiple_of((d ^ s) * rows, rows), rows), :] = weights_in[s][...]

    def col_at(index):
        return pl.ds(pl.multiple_of(index * blk, blk), blk)

    hidden[...] = jnp.zeros_like(hidden)
    zeros = grads.shape[1] // blk // bw

    def product(w, _):
        for k in range(bs):
            q = w * bs + k
            term = jnp.dot(
                tokens[:, col_at(table[slots + q])],
                weights[q],
                preferred_element_type=jnp.float32,
            ).astype(jnp.bfloat16)
            at = col_at(table[2 * slots + q])
            hidden[:, at] = hidden[:, at] + term.astype(jnp.float32)
        return 0

    lax.fori_loop(0, n, product, 0)

    def pointwise(c, _):
        at = col_at(c)
        v = hidden[:, at]
        square = v * v
        t = jnp.tanh(v * (SQRT_2_OVER_PI + (SQRT_2_OVER_PI * 0.044715) * square))
        half = 0.5 + 0.5 * t
        value = v * half
        activated[:, at] = value.astype(jnp.bfloat16)
        slope = half + value * (1.0 - half) * (
            2.0 * SQRT_2_OVER_PI + (6.0 * 0.044715 * SQRT_2_OVER_PI) * square
        )
        slopes[:, at] = (cotangent[:, at].astype(jnp.float32) * slope).astype(jnp.bfloat16)
        for i in range(zeros):
            grads[:, col_at(c * zeros + i)] = jnp.zeros_like(v)
        return 0

    lax.fori_loop(0, bw, pointwise, 0)
    for c in range(bw * zeros, grads.shape[1] // blk):
        grads[:, c * blk : (c + 1) * blk] = jnp.zeros((grads.shape[0], blk), jnp.float32)

    def back(w, _):
        for k in range(bs):
            q = w * bs + k
            term = lax.dot_general(
                slopes[:, col_at(table[2 * slots + q])],
                weights[q],
                (((1,), (1,)), ((), ())),
                preferred_element_type=jnp.float32,
            )
            at = col_at(table[slots + q])
            grads[:, at] = grads[:, at] + term
        return 0

    lax.fori_loop(0, n, back, 0)
    width = own.shape[1]

    def band_of(s):
        band = target_of(me, s, n)
        return grads[:, pl.ds(pl.multiple_of(band * width, blk), width)]

    own[...] = band_of(0)
    for i, s in enumerate(odd):
        relay[i] = band_of(s).astype(jnp.bfloat16)
    for i, s in enumerate(near):
        nears[i][...] = band_of(s).astype(jnp.bfloat16)
    for i, s in enumerate(even):
        evens[i][...] = band_of(s)


def grad_kernel(cfg, here, table, tokens, slopes, *rest):
    n, bs, blk, parts = cfg
    outs = rest[:parts]
    partial = rest[parts]
    slots = n * bs

    def col_at(index):
        return pl.ds(pl.multiple_of(index * blk, blk), blk)

    target = outs[0] if parts == 1 else partial

    def one(w, _):
        for k in range(bs):
            q = w * bs + k
            target[q] = lax.dot_general(
                tokens[:, col_at(table[slots + q])],
                slopes[:, col_at(table[2 * slots + q])],
                (((0,), (0,)), ((), ())),
                preferred_element_type=jnp.float32,
            ).astype(jnp.bfloat16)
        return 0

    lax.fori_loop(0, n, one, 0)
    if parts > 1:
        rows = blk // parts
        d = here[1]
        for s in range(parts):
            outs[s][...] = partial[:, pl.ds(pl.multiple_of((d ^ s) * rows, rows), rows), :]


def pair_kernel(half, *refs):
    for j in range(half):
        total = refs[j][...].astype(jnp.float32) + refs[half + j][...].astype(jnp.float32)
        refs[2 * half + j][...] = total.astype(jnp.bfloat16)


def total_kernel(cfg, here, *rest):
    n, bs, count = cfg
    terms = rest[:count]
    outs = rest[count : count + n]
    pool = rest[count + n]
    me = here[0]
    total = terms[0][...].astype(jnp.float32)
    for term in terms[1:]:
        total = total + term[...].astype(jnp.float32)
    pool[...] = total.astype(jnp.bfloat16)
    for s in range(n):
        band = target_of(me, s, n)
        outs[s][...] = pool[pl.ds(band * bs, bs)]


def adam_kernel(cfg, table, mine, *rest):
    n, per, bs, pad, rows, scale = cfg
    grads = rest[:n]
    moments = rest[n : 2 * n]
    first_out, second_out, weight_out = rest[2 * n : 2 * n + 3]
    pool, moved, grad, weight, first, second = rest[2 * n + 3 :]
    slots = n * bs
    lanes = mine.shape[2]
    for s in range(n):
        pool[s * bs : (s + 1) * bs] = grads[s][...]
        moved[:, s * pad : (s + 1) * pad, :] = moments[s][...]

    for i in range(per):
        grad[i * rows : (i + 1) * rows, :] = (
            pool[table[3 * slots + per + i]].astype(jnp.float32) * scale
        )
        weight[i * rows : (i + 1) * rows, :] = mine[i].astype(jnp.float32)
        at = table[3 * slots + 2 * per + i]
        row = jnp.maximum(at, 0)
        old_first = moved[0, pl.ds(row, 1), :]
        old_second = moved[1, pl.ds(row, 1), :]
        first[i : i + 1, :] = jnp.where(at >= 0, old_first, jnp.zeros_like(old_first))
        second[i : i + 1, :] = jnp.where(at >= 0, old_second, jnp.zeros_like(old_second))

    for r in range(rows):
        at = slice(r * lanes, (r + 1) * lanes)
        strided = pl.ds(r, per, stride=rows)
        g = grad[strided, :]
        first_new = BETA_ONE * first[:, at] + (1.0 - BETA_ONE) * g
        second_new = BETA_TWO * second[:, at] + (1.0 - BETA_TWO) * g * g
        first_out[:, at] = first_new
        second_out[:, at] = second_new
        weight[strided, :] = weight[strided, :] - LEARN_RATE * first_new / (
            jnp.sqrt(second_new) + ADAM_EPSILON
        )
    for i in range(per):
        weight_out[i] = weight[i * rows : (i + 1) * rows, :].astype(jnp.bfloat16)


def flush_kernel(count, *refs):
    sems = refs[2 * count]
    copies = [
        pltpu.make_async_copy(refs[i], refs[count + i], sems.at[i]) for i in range(count)
    ]
    for copy in copies:
        copy.start()
    for copy in copies:
        copy.wait()


def flush(values):
    count = len(values)
    return call(
        functools.partial(flush_kernel, count),
        [shape(x.shape, x.dtype) for x in values],
        [VMEM] * count,
        [pl.BlockSpec(memory_space=pltpu.HBM)] * count,
        [pltpu.SemaphoreType.DMA((count,))],
    )(*values)


def join_kernel(parts, here, *rest):
    out = rest[parts]
    rows = rest[0].shape[1]
    d = here[1]
    for s in range(parts):
        out[:, pl.ds(pl.multiple_of((d ^ s) * rows, rows), rows), :] = rest[s][...]


def split_steps(n):
    steps = list(range(1, n))
    if not paired(n):
        return [], [], steps
    return steps[2::2], steps[:1], steps[1::2]


def relay_kernel(count, *refs):
    evens, outs = refs[:count], refs[-2 * count :]
    half = evens[0].shape[0] // 2
    for i in range(count):
        total = evens[i][...]
        if len(refs) > 3 * count:
            total = total + refs[count][i].astype(jnp.float32)
        total = total.astype(jnp.bfloat16)
        outs[2 * i][...] = total[:half]
        outs[2 * i + 1][...] = total[half:]


def sum_kernel(cfg, own, *rest):
    evens, nears = cfg
    out = rest[-1]
    half = own.shape[0] // 2
    for h in range(2):
        rows = slice(h * half, (h + 1) * half)
        total = own[rows]
        for i in range(evens):
            total = total + rest[2 * i + h][...].astype(jnp.float32)
        for i in range(nears):
            total = total + rest[2 * evens + i][rows].astype(jnp.float32)
        out[rows] = total.astype(jnp.bfloat16)


def swap(value, bits, parts):
    return lax.ppermute(value, "dp", [(i, i ^ bits) for i in range(parts)])


def shift(value, step, n):
    return lax.ppermute(value, "mp", [(i, target_of_static(i, step, n)) for i in range(n)])


def plane_gather(value, parts):
    pieces = [value] + [None] * (parts - 1)
    for s in range(2, parts, 2):
        pieces[s] = swap(value, s, parts)
    for s in range(0, parts, 2):
        pieces[s + 1] = swap(pieces[s], 1, parts)
    return pieces


def step(tokens_in, cotangent, old_weights, old_first, old_second, new_coords, moved_to):
    n = lax.axis_size("mp")
    parts = lax.axis_size("dp")
    me = lax.axis_index("mp")
    d = lax.axis_index("dp")
    cap, blk = old_weights.shape[:2]
    total = new_coords.shape[0]
    per = total // n
    shard = old_first.shape[1]
    rows = blk // parts
    tok, width = tokens_in.shape
    bw = cotangent.shape[1] // blk
    ms = cap // n
    pad = -(-ms // 8) * 8
    bs = 2 * per // n + 1
    slots = n * bs
    direct = rows % 16 == 0 and parts & (parts - 1) == 0
    bf16, f32 = jnp.bfloat16, jnp.float32
    here = jnp.stack([me, d]).astype(jnp.int32)

    share = call(
        share_kernel, shape((cap, rows, blk), bf16), [ANY], VMEM, [pltpu.SemaphoreType.DMA(())]
    )(in_hbm(old_weights))
    shares = [share] + [shift(share, s, n) for s in range(1, n)]

    out = 3 * slots + 3 * per
    table = call(
        functools.partial(plan_kernel, (n, per, cap, ms, bs, bw, pad)),
        shape((out + n * ms + 4,), jnp.int32),
        [SMEM] * 3,
        SMEM,
        [pltpu.SMEM((total + 8,), jnp.int32)],
    )(here, in_hbm(new_coords.T), in_hbm(moved_to))

    picked, mine = call(
        functools.partial(select_kernel, (n, per, cap, bs)),
        [shape((slots, rows, blk), bf16), shape((per, rows, blk), bf16)],
        [SMEM] + [VMEM] * n,
        [VMEM, VMEM],
        [pltpu.VMEM((n * cap, rows, blk), bf16)],
    )(table, *shares)

    if direct:
        pieces = plane_gather(picked, parts)
    else:
        gathered = lax.all_gather(picked, "dp", axis=0)
        pieces = [gathered.transpose(1, 0, 2, 3).reshape(slots, blk, blk)]

    packed = call(
        functools.partial(pack_kernel, (n, ms, pad, out)),
        [shape((2, pad, shard), f32)] * n
        + [shape(tokens_in.shape, bf16), shape(cotangent.shape, bf16)],
        [SMEM] + [ANY] * 4,
        [VMEM] * (n + 2),
        [
            pltpu.VMEM(old_first.shape, f32),
            pltpu.VMEM(old_second.shape, f32),
            pltpu.SemaphoreType.DMA((4,)),
        ],
    )(table, *[in_hbm(x) for x in (old_first, old_second, tokens_in, cotangent)])
    packs = packed[:n]
    tokens, cotangents = packed[n:]
    moments = [packs[0]] + [shift(packs[s], s, n) for s in range(1, n)]

    odd, near, even = split_steps(n)
    results = call(
        functools.partial(forward_kernel, (n, bs, bw, blk, len(pieces))),
        [pltpu.VMEM((tok, bw * blk), bf16), shape((tok, bw * blk), bf16)]
        + [shape((len(odd), tok, width // n), bf16)] * min(len(odd), 1)
        + [shape((tok, width // n), bf16)] * len(near)
        + [shape((tok, width // n), f32)] * (len(even) + 1),
        [SMEM, SMEM, VMEM, VMEM] + [VMEM] * len(pieces),
        [VMEM] * (3 + min(len(odd), 1) + len(near) + len(even)),
        [
            pltpu.VMEM((slots, blk, blk), bf16),
            pltpu.VMEM((tok, bw * blk), f32),
            pltpu.VMEM((tok, width), f32),
        ],
    )(here, table, tokens, cotangents, *pieces)
    activated, slopes = results[:2]
    rest = list(results[2:])
    relayed = [shift(rest.pop(0), 1, n)] if odd else []
    nears = [rest.pop(0) for _ in near]
    evens, own = rest[:-1], rest[-1]

    count = parts if direct else 1
    partials = call(
        functools.partial(grad_kernel, (n, bs, blk, count)),
        [shape((slots, blk // count, blk), bf16)] * count,
        [SMEM, SMEM, VMEM, VMEM],
        [VMEM] * count,
        [pltpu.VMEM((slots, blk, blk), bf16)],
    )(here, table, tokens, slopes)

    halves = call(
        functools.partial(relay_kernel, len(even)),
        [shape((tok // 2, width // n), bf16)] * (2 * len(even)),
        [VMEM] * (len(even) + len(relayed)),
        [VMEM] * (2 * len(even)),
        [],
    )(*evens, *relayed)
    back_terms = []
    for i, s in enumerate(even):
        back_terms += [shift(halves[2 * i + h], s, n) for h in range(2)]
    back_terms += [shift(x, s, n) for x, s in zip(nears, near)]

    if direct:
        half = parts // 2
        kept = [partials[2 * j] for j in range(half)]
        crossed = [swap(partials[2 * j + 1], 1, parts) for j in range(half)]
        summed = call(
            functools.partial(pair_kernel, half),
            [shape((slots, rows, blk), bf16)] * half,
            [VMEM] * parts,
            [VMEM] * half,
            [],
        )(*kept, *crossed)
        terms = [summed[0]] + [swap(summed[j], 2 * j, parts) for j in range(1, half)]
    else:
        spread = partials[0].reshape(slots, parts, rows, blk).transpose(1, 0, 2, 3)
        spread = lax.all_to_all(spread, "dp", split_axis=0, concat_axis=0, tiled=True)
        terms = [jnp.sum(spread.astype(f32), axis=0)]

    owner_grads = call(
        functools.partial(total_kernel, (n, bs, len(terms))),
        [shape((bs, rows, blk), bf16)] * n,
        [SMEM] + [VMEM] * len(terms),
        [VMEM] * n,
        [pltpu.VMEM((slots, rows, blk), bf16)],
    )(here, *terms)
    arrived = [owner_grads[0]] + [shift(owner_grads[s], s, n) for s in range(1, n)]

    first_new, second_new, weight_share = call(
        functools.partial(
            adam_kernel, (n, per, bs, pad, rows, 1.0 / math.sqrt(tok * parts))
        ),
        [pltpu.VMEM((per, shard), f32)] * 2 + [shape((per, rows, blk), bf16)],
        [SMEM, VMEM] + [VMEM] * (2 * n),
        [VMEM] * 3,
        [
            pltpu.VMEM((slots, rows, blk), bf16),
            pltpu.VMEM((2, n * pad, shard), f32),
            pltpu.VMEM((per * rows, blk), f32),
            pltpu.VMEM((per * rows, blk), f32),
            pltpu.VMEM((per, shard), f32),
            pltpu.VMEM((per, shard), f32),
        ],
    )(table, mine, *arrived, *moments)

    if direct:
        weights_out = call(
            functools.partial(join_kernel, parts),
            shape((per, blk, blk), bf16),
            [SMEM] + [VMEM] * parts,
            VMEM,
            [],
        )(here, *plane_gather(weight_share, parts))
    else:
        weights_out = lax.all_gather(weight_share, "dp", axis=1, tiled=True)

    grad_inputs = call(
        functools.partial(sum_kernel, (len(even), len(near))),
        shape((tok, width // n), bf16),
        [VMEM] * (1 + len(back_terms)),
        VMEM,
        [],
    )(own, *back_terms)
    (activated,) = flush([activated])
    first_new, second_new = flush([first_new, second_new])
    return (activated, grad_inputs, weights_out, first_new, second_new)


def solution(mesh):
    in_specs = (
        P("dp", None),
        P("dp", "mp"),
        P("mp", None, None),
        P("mp", "dp"),
        P("mp", "dp"),
        P(),
        P(),
    )
    out_specs = (P("dp", "mp"), P("dp", "mp"), P("mp", None, None), P("mp", "dp"), P("mp", "dp"))
    return jax.shard_map(step, mesh=mesh, in_specs=in_specs, out_specs=out_specs, check_vma=False)
```

```python
import functools
import math

import jax
import jax.numpy as jnp
from jax import lax
from jax.experimental import pallas as pl
from jax.experimental.pallas import tpu as pltpu
from jax.sharding import PartitionSpec as P


BETA_ONE = 0.9
BETA_TWO = 0.95
LEARN_RATE = 0.01
ADAM_EPSILON = 0.05
SQRT_2_OVER_PI = math.sqrt(2.0 / math.pi)


ROOM_BYTES = 4 << 20

VMEM = pl.BlockSpec(memory_space=pltpu.VMEM)
SMEM = pl.BlockSpec(memory_space=pltpu.SMEM)
ANY = pl.BlockSpec(memory_space=pl.ANY)


def in_hbm(value):
    return pltpu.with_memory_space_constraint(value, pltpu.HBM)


def size_of(item):
    return math.prod(item.shape) * jnp.dtype(item.dtype).itemsize


def call(kernel, out_shape, in_specs, out_specs, scratch):
    def run(*args):
        outs = out_shape if isinstance(out_shape, list) else [out_shape]
        held = [x for x in scratch if hasattr(x, "shape") and x.dtype in (jnp.int32, jnp.bfloat16, jnp.float32)]
        room = sum(size_of(x) for x in (*args, *outs, *held))
        return pl.pallas_call(
            kernel,
            out_shape=out_shape,
            in_specs=in_specs,
            out_specs=out_specs,
            scratch_shapes=scratch,
            compiler_params=pltpu.CompilerParams(vmem_limit_bytes=room + ROOM_BYTES),
        )(*args)

    return run


def shape(dims, dtype):
    return jax.ShapeDtypeStruct(dims, dtype)


def paired(n):
    return n & (n - 1) == 0


def rel_to(me, other, n):
    if paired(n):
        return me ^ other
    rel = other - me
    return jnp.where(rel < 0, rel + n, rel)


def rel_from(me, other, n):
    if paired(n):
        return me ^ other
    rel = me - other
    return jnp.where(rel < 0, rel + n, rel)


def target_of(me, step, n):
    if paired(n):
        return me ^ step
    other = me + step
    return jnp.where(other >= n, other - n, other)


def target_of_static(i, step, n):
    return i ^ step if paired(n) else (i + step) % n


def which_group(value, group, count):
    found = jnp.int32(0)
    for edge in range(1, count):
        found = found + (value >= edge * group).astype(jnp.int32)
    return found


def take_rank(counts, at, live):
    rank = jnp.int32(0)
    new = []
    for i, count in enumerate(counts):
        hit = jnp.where(jnp.logical_and(live, at == i), 1, 0)
        rank = rank + hit * count
        new.append(count + hit)
    return rank, tuple(new)


def plan_kernel(cfg, here, coords, moved, *rest):
    n, per, cap, ms, bs, bw, pad = cfg
    sources, table, targets, src, sems = rest[:4], rest[4], rest[5:9], rest[9], rest[10]
    copies = [
        pltpu.make_async_copy(sources[i], targets[i], sems.at[i]) for i in range(len(sources))
    ]
    for copy in copies:
        copy.start()
    total = n * per
    slots = n * bs
    share, grad, moment = 3 * slots, 3 * slots + per, 3 * slots + 2 * per
    out = moment + per
    spare = out + n * ms
    me = here[0]

    def fill(ref, base, size, value):
        def put(i, _):
            ref[base + i] = jnp.int32(value)
            return 0

        lax.fori_loop(0, size, put, 0, unroll=math.gcd(size, 4))

    fill(src, 0, total, -1)
    fill(table, 0, slots, -1)
    fill(table, slots, 2 * slots, 0)
    fill(table, moment, per, -1)
    fill(table, out, n * ms, 0)
    zeros = (jnp.int32(0),) * n

    for p in range(n):
        rel = rel_from(me, p, n)

        def old_slot(j, counts):
            t = moved[p * cap + j]
            live = t >= 0
            dest = which_group(t, per, n)
            k, counts = take_rank(counts, dest, live)
            src[jnp.where(live, t, total)] = rel * cap + j
            gone = jnp.logical_and(live, me == p)
            table[jnp.where(gone, out + rel_to(me, dest, n) * ms + k, spare)] = j
            came = jnp.logical_and(live, dest == me)
            table[jnp.where(came, moment + t - me * per, spare)] = rel * pad + k
            return counts

        lax.fori_loop(0, cap, old_slot, zeros, unroll=math.gcd(cap, 4))

    for w in range(n):

        def new_slot(j, counts):
            b = w * per + j
            row = coords[0, b]
            col = coords[1, b]
            source = src[b]
            band = which_group(col, bw, n)
            k, counts = take_rank(counts, band, True)
            q = w * bs + k
            near = band == me
            table[jnp.where(near, q, spare)] = source
            table[jnp.where(near, slots + q, spare)] = row
            table[jnp.where(near, 2 * slots + q, spare)] = col - me * bw
            own = me == w
            table[jnp.where(own, share + j, spare)] = source
            table[jnp.where(own, grad + j, spare)] = rel_from(me, band, n) * bs + k
            return counts

        lax.fori_loop(0, per, new_slot, zeros, unroll=math.gcd(per, 4))

    for copy in copies:
        copy.wait()


def pack_kernel(cfg, table, first, second, *packs):
    n, ms, pad, out = cfg
    for s in range(n):
        for k in range(ms):
            row = table[out + s * ms + k]
            packs[s][0, k : k + 1, :] = first[pl.ds(row, 1), :]
            packs[s][1, k : k + 1, :] = second[pl.ds(row, 1), :]
        if pad > ms:
            packs[s][:, ms:pad, :] = jnp.zeros((2, pad - ms, first.shape[1]), jnp.float32)


def share_kernel(weights, out, sem):
    rows = out.shape[1]
    at = pl.multiple_of(lax.axis_index("dp") * rows, rows)
    copy = pltpu.make_async_copy(weights.at[:, pl.ds(at, rows), :], out, sem)
    copy.start()
    copy.wait()


def select_kernel(cfg, table, *rest):
    n, per, cap, bs = cfg
    shares = rest[:n]
    picked, mine, pool = rest[n:]
    slots = n * bs
    for s in range(n):
        pool[s * cap : (s + 1) * cap] = shares[s][...]

    def pick(out, base):
        def one(i, _):
            at = table[base + i]
            row = pool[jnp.maximum(at, 0)]
            out[i] = jnp.where(at >= 0, row, jnp.zeros_like(row))
            return 0

        return one

    lax.fori_loop(0, slots, pick(picked, 0), 0, unroll=4)
    lax.fori_loop(0, per, pick(mine, 3 * slots), 0, unroll=4)


def forward_kernel(cfg, here, table, tokens, cotangent, *rest):
    n, bs, bw, blk, parts = cfg
    weights_in = rest[:parts]
    rest = rest[parts:]
    activated, slopes = rest[:2]
    odd, near, even = split_steps(n)
    relay = rest[2] if odd else None
    at = 2 + (1 if odd else 0)
    nears = rest[at : at + len(near)]
    at += len(near)
    evens = rest[at : at + len(even)]
    own, weights, hidden, grads = rest[at + len(even) :]
    slots = n * bs
    me = here[0]
    if parts == 1:
        weights = weights_in[0]
    else:
        rows = blk // parts
        d = here[1]
        for s in range(parts):
            weights[:, pl.ds(pl.multiple_of((d ^ s) * rows, rows), rows), :] = weights_in[s][...]

    def col_at(index):
        return pl.ds(pl.multiple_of(index * blk, blk), blk)

    hidden[...] = jnp.zeros_like(hidden)
    zeros = grads.shape[1] // blk // bw

    def product(w, _):
        for k in range(bs):
            q = w * bs + k
            term = jnp.dot(
                tokens[:, col_at(table[slots + q])],
                weights[q],
                preferred_element_type=jnp.float32,
            ).astype(jnp.bfloat16)
            at = col_at(table[2 * slots + q])
            hidden[:, at] = hidden[:, at] + term.astype(jnp.float32)
        return 0

    lax.fori_loop(0, n, product, 0)

    def pointwise(c, _):
        at = col_at(c)
        v = hidden[:, at]
        square = v * v
        t = jnp.tanh(v * (SQRT_2_OVER_PI + (SQRT_2_OVER_PI * 0.044715) * square))
        half = 0.5 + 0.5 * t
        value = v * half
        activated[:, at] = value.astype(jnp.bfloat16)
        slope = half + value * (1.0 - half) * (
            2.0 * SQRT_2_OVER_PI + (6.0 * 0.044715 * SQRT_2_OVER_PI) * square
        )
        slopes[:, at] = (cotangent[:, at].astype(jnp.float32) * slope).astype(jnp.bfloat16)
        for i in range(zeros):
            grads[:, col_at(c * zeros + i)] = jnp.zeros_like(v)
        return 0

    lax.fori_loop(0, bw, pointwise, 0)
    for c in range(bw * zeros, grads.shape[1] // blk):
        grads[:, c * blk : (c + 1) * blk] = jnp.zeros((grads.shape[0], blk), jnp.float32)

    def back(w, _):
        for k in range(bs):
            q = w * bs + k
            term = lax.dot_general(
                slopes[:, col_at(table[2 * slots + q])],
                weights[q],
                (((1,), (1,)), ((), ())),
                preferred_element_type=jnp.float32,
            )
            at = col_at(table[slots + q])
            grads[:, at] = grads[:, at] + term
        return 0

    lax.fori_loop(0, n, back, 0)
    width = own.shape[1]

    def band_of(s):
        band = target_of(me, s, n)
        return grads[:, pl.ds(pl.multiple_of(band * width, blk), width)]

    own[...] = band_of(0)
    for i, s in enumerate(odd):
        relay[i] = band_of(s).astype(jnp.bfloat16)
    for i, s in enumerate(near):
        nears[i][...] = band_of(s).astype(jnp.bfloat16)
    for i, s in enumerate(even):
        evens[i][...] = band_of(s)


def grad_kernel(cfg, here, table, tokens, slopes, *rest):
    n, bs, blk, parts = cfg
    outs = rest[:parts]
    partial = rest[parts]
    slots = n * bs

    def col_at(index):
        return pl.ds(pl.multiple_of(index * blk, blk), blk)

    target = outs[0] if parts == 1 else partial

    def one(w, _):
        for k in range(bs):
            q = w * bs + k
            target[q] = lax.dot_general(
                tokens[:, col_at(table[slots + q])],
                slopes[:, col_at(table[2 * slots + q])],
                (((0,), (0,)), ((), ())),
                preferred_element_type=jnp.float32,
            ).astype(jnp.bfloat16)
        return 0

    lax.fori_loop(0, n, one, 0)
    if parts > 1:
        rows = blk // parts
        d = here[1]
        for s in range(parts):
            outs[s][...] = partial[:, pl.ds(pl.multiple_of((d ^ s) * rows, rows), rows), :]


def pair_kernel(half, *refs):
    for j in range(half):
        total = refs[j][...].astype(jnp.float32) + refs[half + j][...].astype(jnp.float32)
        refs[2 * half + j][...] = total.astype(jnp.bfloat16)


def total_kernel(cfg, here, *rest):
    n, bs, count = cfg
    terms = rest[:count]
    outs = rest[count : count + n]
    pool = rest[count + n]
    me = here[0]
    total = terms[0][...].astype(jnp.float32)
    for term in terms[1:]:
        total = total + term[...].astype(jnp.float32)
    pool[...] = total.astype(jnp.bfloat16)
    for s in range(n):
        band = target_of(me, s, n)
        outs[s][...] = pool[pl.ds(band * bs, bs)]


def adam_kernel(cfg, table, mine, *rest):
    n, per, bs, pad, rows, scale = cfg
    grads = rest[:n]
    moments = rest[n : 2 * n]
    first_out, second_out, weight_out = rest[2 * n : 2 * n + 3]
    pool, moved, grad, weight, first, second = rest[2 * n + 3 :]
    slots = n * bs
    lanes = mine.shape[2]
    for s in range(n):
        pool[s * bs : (s + 1) * bs] = grads[s][...]
        moved[:, s * pad : (s + 1) * pad, :] = moments[s][...]

    for i in range(per):
        grad[i * rows : (i + 1) * rows, :] = (
            pool[table[3 * slots + per + i]].astype(jnp.float32) * scale
        )
        weight[i * rows : (i + 1) * rows, :] = mine[i].astype(jnp.float32)
        at = table[3 * slots + 2 * per + i]
        row = jnp.maximum(at, 0)
        old_first = moved[0, pl.ds(row, 1), :]
        old_second = moved[1, pl.ds(row, 1), :]
        first[i : i + 1, :] = jnp.where(at >= 0, old_first, jnp.zeros_like(old_first))
        second[i : i + 1, :] = jnp.where(at >= 0, old_second, jnp.zeros_like(old_second))

    for r in range(rows):
        at = slice(r * lanes, (r + 1) * lanes)
        strided = pl.ds(r, per, stride=rows)
        g = grad[strided, :]
        first_new = BETA_ONE * first[:, at] + (1.0 - BETA_ONE) * g
        second_new = BETA_TWO * second[:, at] + (1.0 - BETA_TWO) * g * g
        first_out[:, at] = first_new
        second_out[:, at] = second_new
        weight[strided, :] = weight[strided, :] - LEARN_RATE * first_new / (
            jnp.sqrt(second_new) + ADAM_EPSILON
        )
    for i in range(per):
        weight_out[i] = weight[i * rows : (i + 1) * rows, :].astype(jnp.bfloat16)


def flush_kernel(count, *refs):
    sems = refs[2 * count]
    copies = [
        pltpu.make_async_copy(refs[i], refs[count + i], sems.at[i]) for i in range(count)
    ]
    for copy in copies:
        copy.start()
    for copy in copies:
        copy.wait()


def flush(values):
    count = len(values)
    return call(
        functools.partial(flush_kernel, count),
        [shape(x.shape, x.dtype) for x in values],
        [VMEM] * count,
        [pl.BlockSpec(memory_space=pltpu.HBM)] * count,
        [pltpu.SemaphoreType.DMA((count,))],
    )(*values)


def join_kernel(parts, here, *rest):
    out = rest[parts]
    rows = rest[0].shape[1]
    d = here[1]
    for s in range(parts):
        out[:, pl.ds(pl.multiple_of((d ^ s) * rows, rows), rows), :] = rest[s][...]


def split_steps(n):
    steps = list(range(1, n))
    if not paired(n):
        return [], [], steps
    return steps[2::2], steps[:1], steps[1::2]


def relay_kernel(count, *refs):
    evens, outs = refs[:count], refs[-2 * count :]
    half = evens[0].shape[0] // 2
    for i in range(count):
        total = evens[i][...]
        if len(refs) > 3 * count:
            total = total + refs[count][i].astype(jnp.float32)
        total = total.astype(jnp.bfloat16)
        outs[2 * i][...] = total[:half]
        outs[2 * i + 1][...] = total[half:]


def sum_kernel(cfg, own, *rest):
    evens, nears = cfg
    out = rest[-1]
    half = own.shape[0] // 2
    for h in range(2):
        rows = slice(h * half, (h + 1) * half)
        total = own[rows]
        for i in range(evens):
            total = total + rest[2 * i + h][...].astype(jnp.float32)
        for i in range(nears):
            total = total + rest[2 * evens + i][rows].astype(jnp.float32)
        out[rows] = total.astype(jnp.bfloat16)


def swap(value, bits, parts):
    return lax.ppermute(value, "dp", [(i, i ^ bits) for i in range(parts)])


def shift(value, step, n):
    return lax.ppermute(value, "mp", [(i, target_of_static(i, step, n)) for i in range(n)])


def plane_gather(value, parts):
    pieces = [value] + [None] * (parts - 1)
    for s in range(2, parts, 2):
        pieces[s] = swap(value, s, parts)
    for s in range(0, parts, 2):
        pieces[s + 1] = swap(pieces[s], 1, parts)
    return pieces


def step(tokens_in, cotangent, old_weights, old_first, old_second, new_coords, moved_to):
    n = lax.axis_size("mp")
    parts = lax.axis_size("dp")
    me = lax.axis_index("mp")
    d = lax.axis_index("dp")
    cap, blk = old_weights.shape[:2]
    total = new_coords.shape[0]
    per = total // n
    shard = old_first.shape[1]
    rows = blk // parts
    tok, width = tokens_in.shape
    bw = cotangent.shape[1] // blk
    ms = cap // n
    pad = -(-ms // 8) * 8
    bs = 2 * per // n + 1
    slots = n * bs
    direct = rows % 16 == 0 and parts & (parts - 1) == 0
    bf16, f32 = jnp.bfloat16, jnp.float32
    here = jnp.stack([me, d]).astype(jnp.int32)

    share = call(
        share_kernel, shape((cap, rows, blk), bf16), [ANY], VMEM, [pltpu.SemaphoreType.DMA(())]
    )(in_hbm(old_weights))
    shares = [share] + [shift(share, s, n) for s in range(1, n)]

    out = 3 * slots + 3 * per
    big = (old_first, old_second, tokens_in, cotangent)
    table, first, second, tokens, cotangents = call(
        functools.partial(plan_kernel, (n, per, cap, ms, bs, bw, pad)),
        [shape((out + n * ms + 4,), jnp.int32)] + [shape(x.shape, x.dtype) for x in big],
        [SMEM] * 3 + [ANY] * 4,
        [SMEM] + [VMEM] * 4,
        [pltpu.SMEM((total + 8,), jnp.int32), pltpu.SemaphoreType.DMA((4,))],
    )(here, *[in_hbm(x) for x in (new_coords.T, moved_to, *big)])

    picked, mine = call(
        functools.partial(select_kernel, (n, per, cap, bs)),
        [shape((slots, rows, blk), bf16), shape((per, rows, blk), bf16)],
        [SMEM] + [VMEM] * n,
        [VMEM, VMEM],
        [pltpu.VMEM((n * cap, rows, blk), bf16)],
    )(table, *shares)

    if direct:
        pieces = plane_gather(picked, parts)
    else:
        gathered = lax.all_gather(picked, "dp", axis=0)
        pieces = [gathered.transpose(1, 0, 2, 3).reshape(slots, blk, blk)]

    packs = call(
        functools.partial(pack_kernel, (n, ms, pad, out)),
        [shape((2, pad, shard), f32)] * n,
        [SMEM] + [VMEM] * 2,
        [VMEM] * n,
        [],
    )(table, first, second)
    moments = [packs[0]] + [shift(packs[s], s, n) for s in range(1, n)]

    odd, near, even = split_steps(n)
    results = call(
        functools.partial(forward_kernel, (n, bs, bw, blk, len(pieces))),
        [pltpu.VMEM((tok, bw * blk), bf16), shape((tok, bw * blk), bf16)]
        + [shape((len(odd), tok, width // n), bf16)] * min(len(odd), 1)
        + [shape((tok, width // n), bf16)] * len(near)
        + [shape((tok, width // n), f32)] * (len(even) + 1),
        [SMEM, SMEM, VMEM, VMEM] + [VMEM] * len(pieces),
        [VMEM] * (3 + min(len(odd), 1) + len(near) + len(even)),
        [
            pltpu.VMEM((slots, blk, blk), bf16),
            pltpu.VMEM((tok, bw * blk), f32),
            pltpu.VMEM((tok, width), f32),
        ],
    )(here, table, tokens, cotangents, *pieces)
    activated, slopes = results[:2]
    rest = list(results[2:])
    relayed = [shift(rest.pop(0), 1, n)] if odd else []
    nears = [rest.pop(0) for _ in near]
    evens, own = rest[:-1], rest[-1]

    count = parts if direct else 1
    partials = call(
        functools.partial(grad_kernel, (n, bs, blk, count)),
        [shape((slots, blk // count, blk), bf16)] * count,
        [SMEM, SMEM, VMEM, VMEM],
        [VMEM] * count,
        [pltpu.VMEM((slots, blk, blk), bf16)],
    )(here, table, tokens, slopes)

    halves = call(
        functools.partial(relay_kernel, len(even)),
        [shape((tok // 2, width // n), bf16)] * (2 * len(even)),
        [VMEM] * (len(even) + len(relayed)),
        [VMEM] * (2 * len(even)),
        [],
    )(*evens, *relayed)
    back_terms = []
    for i, s in enumerate(even):
        back_terms += [shift(halves[2 * i + h], s, n) for h in range(2)]
    back_terms += [shift(x, s, n) for x, s in zip(nears, near)]

    if direct:
        half = parts // 2
        kept = [partials[2 * j] for j in range(half)]
        crossed = [swap(partials[2 * j + 1], 1, parts) for j in range(half)]
        summed = call(
            functools.partial(pair_kernel, half),
            [shape((slots, rows, blk), bf16)] * half,
            [VMEM] * parts,
            [VMEM] * half,
            [],
        )(*kept, *crossed)
        terms = [summed[0]] + [swap(summed[j], 2 * j, parts) for j in range(1, half)]
    else:
        spread = partials[0].reshape(slots, parts, rows, blk).transpose(1, 0, 2, 3)
        spread = lax.all_to_all(spread, "dp", split_axis=0, concat_axis=0, tiled=True)
        terms = [jnp.sum(spread.astype(f32), axis=0)]

    owner_grads = call(
        functools.partial(total_kernel, (n, bs, len(terms))),
        [shape((bs, rows, blk), bf16)] * n,
        [SMEM] + [VMEM] * len(terms),
        [VMEM] * n,
        [pltpu.VMEM((slots, rows, blk), bf16)],
    )(here, *terms)
    arrived = [owner_grads[0]] + [shift(owner_grads[s], s, n) for s in range(1, n)]

    first_new, second_new, weight_share = call(
        functools.partial(
            adam_kernel, (n, per, bs, pad, rows, 1.0 / math.sqrt(tok * parts))
        ),
        [pltpu.VMEM((per, shard), f32)] * 2 + [shape((per, rows, blk), bf16)],
        [SMEM, VMEM] + [VMEM] * (2 * n),
        [VMEM] * 3,
        [
            pltpu.VMEM((slots, rows, blk), bf16),
            pltpu.VMEM((2, n * pad, shard), f32),
            pltpu.VMEM((per * rows, blk), f32),
            pltpu.VMEM((per * rows, blk), f32),
            pltpu.VMEM((per, shard), f32),
            pltpu.VMEM((per, shard), f32),
        ],
    )(table, mine, *arrived, *moments)

    if direct:
        weights_out = call(
            functools.partial(join_kernel, parts),
            shape((per, blk, blk), bf16),
            [SMEM] + [VMEM] * parts,
            VMEM,
            [],
        )(here, *plane_gather(weight_share, parts))
    else:
        weights_out = lax.all_gather(weight_share, "dp", axis=1, tiled=True)

    grad_inputs = call(
        functools.partial(sum_kernel, (len(even), len(near))),
        shape((tok, width // n), bf16),
        [VMEM] * (1 + len(back_terms)),
        VMEM,
        [],
    )(own, *back_terms)
    (activated,) = flush([activated])
    first_new, second_new = flush([first_new, second_new])
    return (activated, grad_inputs, weights_out, first_new, second_new)


def solution(mesh):
    in_specs = (
        P("dp", None),
        P("dp", "mp"),
        P("mp", None, None),
        P("mp", "dp"),
        P("mp", "dp"),
        P(),
        P(),
    )
    out_specs = (P("dp", "mp"), P("dp", "mp"), P("mp", None, None), P("mp", "dp"), P("mp", "dp"))
    return jax.shard_map(step, mesh=mesh, in_specs=in_specs, out_specs=out_specs, check_vma=False)
```
